512 devices in a mesh: fsdp: 8 (over z_hi, x), ctx: 16 (over y, core), tp: 4 (over z_lo).
Axes of the slice: x: 4, y: 8, z: 8 (z_hi: 2, z_lo: 4; z = z_hi * 4 + z_lo), core: 2. Of those that a mesh axis runs over, the one named last changes fastest.
Arguments:
- q_in: bfloat16 [8, 4096, 4096], P('fsdp', 'ctx', 'tp'), may hold values from -6 to 6
- k_in: bfloat16 [8, 4096, 4096], P('fsdp', 'ctx', 'tp'), may hold values from -6 to 6
- v_in: bfloat16 [8, 4096, 4096], P('fsdp', 'ctx', 'tp'), may hold values from -6 to 6
- grad_out: bfloat16 [8, 4096, 4096], P('fsdp', 'ctx', 'tp'), may hold values from -6 to 6
- genome_ids: int32 [8, 4096], P('fsdp', 'ctx'), may hold values from 0 to 31, never falling along the last dimension, each value on 1 to 1024 neighbouring positions
- long_filter: bfloat16 [256, 128], P('tp', 'fsdp'), may hold values from -0.5 to 0.5
- short_filter: float32 [3, 7, 4096], P(None, None, 'tp'), may hold values from -2 to 2
Outputs:
- grad_q: bfloat16 [8, 4096, 4096], P('fsdp', 'ctx', 'tp')
- grad_k: bfloat16 [8, 4096, 4096], P('fsdp', 'ctx', 'tp')
- grad_v: bfloat16 [8, 4096, 4096], P('fsdp', 'ctx', 'tp')
- grad_long: float32 [256, 128], P('tp', 'fsdp')
- grad_short: float32 [3, 7, 4096], P(None, None, 'tp')
The draws below stay inside these ranges and needn't reach their ends.
Inputs may be any that keep to these rules, and one draw needn't show every extreme that they name: `genome_ids`: along each sequence the genome ids never fall; each genome covers 1 to 1024 positions, and one covers exactly that many.
All inputs are finite; a program needn't handle non-finite values.
Results may differ from the reference program's by a relative error of at most 0.005.
Values may be sent and summed in bfloat16 or wider, within the bound.
A program may use at most 128 MiB of HBM per device.

```python
import math
import jax
import jax.numpy as jnp
import numpy as np
from jax import lax

CH = 4096
GROUP = 16
TAPS = 128
SHORT = 7
LEN = 4096
SEQS = 8
GROUPS = 256
GENOMES = 32


def levels(stream_key, extent, shards, least, top_value):
    gain = 1.0
    for dim, parts in shards:
        draws = jax.random.uniform(jax.random.fold_in(jax.random.fold_in(stream_key, 6), dim), (parts,), jnp.float32, least / len(shards), top_value / len(shards))
        gain = gain * jnp.repeat(jnp.exp(draws), extent[dim] // parts).reshape((-1,) + (1,) * (len(extent) - 1 - dim))
    return gain


def length_profile(count, total, most, slope):
    portions = [(1 << 20) // math.isqrt(grade ** slope) + 1 for grade in range(2, count + 1)]
    rest, holding = total - most - (count - 1), [1] * (count - 1)
    while rest > 0:
        candidates = [i for i in range(count - 1) if holding[i] < most]
        mass, budget = sum([portions[i] for i in candidates]), rest
        for i in candidates:
            extra = min(most - holding[i], max(1, budget * portions[i] // mass), rest)
            holding[i] = holding[i] + extra
            rest = rest - extra
    return np.array([most] + holding)


def uneven_parts(rng, number_of, total, most, skew):
    if number_of == 2:
        one = jax.random.randint(rng, (), max(1, total - most), min(most, total - 1) + 1)
        return jnp.stack([one, total - one])
    lengths = jnp.asarray(length_profile(number_of, total, most, skew), jnp.int32)
    pairs = (number_of - 1) // 2
    giver, receiver = lengths[1:1 + 2 * pairs:2], lengths[2:2 + 2 * pairs:2]
    margin = jnp.minimum(giver - 1, most - receiver)
    shifted = jax.random.randint(jax.random.fold_in(rng, 1), (pairs,), 0, 1 << 20) % (margin + 1)
    lengths = lengths.at[1:1 + 2 * pairs:2].set(giver - shifted).at[2:2 + 2 * pairs:2].set(receiver + shifted)
    return lengths[jax.random.permutation(jax.random.fold_in(rng, 2), number_of)]


def bell_draw(rng, shape, deviation, bound, pieces=(), held_as=jnp.bfloat16):
    loudness = levels(rng, shape, pieces, -0.22, 0.18) if pieces else 1.0
    array = jax.random.normal(rng, shape, jnp.float32) * deviation * loudness
    return jnp.minimum(jnp.maximum(array, -bound), bound).astype(held_as)


def setup_inputs(seed: int = 0) -> dict:
    seeds = jax.random.split(jax.random.key(seed), 8)
    q_in = bell_draw(seeds[0], (SEQS, LEN, CH), 1.0, 6.0, ((0, 8), (1, 16), (2, 4)))
    k_in = bell_draw(seeds[1], (SEQS, LEN, CH), 1.0, 6.0, ((0, 8), (1, 16), (2, 4)))
    v_in = bell_draw(seeds[2], (SEQS, LEN, CH), 1.0, 6.0, ((0, 8), (1, 16), (2, 4)))
    grad_out = bell_draw(seeds[3], (SEQS, LEN, CH), 1.0, 6.0, ((0, 8), (1, 16), (2, 4)))
    genome_ids = jax.vmap(lambda own: jnp.searchsorted(jnp.cumsum(uneven_parts(own, GENOMES, LEN, LEN // 4, 1)), jnp.arange(LEN), side="right"))(jax.random.split(seeds[4], SEQS)).reshape((SEQS, LEN)).astype(jnp.int32)
    long_filter = bell_draw(seeds[5], (GROUPS, TAPS), TAPS ** -0.5, 0.5, ((0, 4), (1, 8)))
    short_filter = bell_draw(seeds[6], (3, SHORT, CH), SHORT ** -0.5, 2.0, ((2, 4),), jnp.float32)
    return {"q_in": q_in, "k_in": k_in, "v_in": v_in, "grad_out": grad_out, "genome_ids": genome_ids, "long_filter": long_filter, "short_filter": short_filter}


def toeplitz_band(filters, causal):
    group_count, tap_count = filters.shape
    if causal:
        pattern = jnp.concatenate([jnp.zeros((group_count, 1), filters.dtype), filters[:, ::-1], jnp.zeros((group_count, tap_count), filters.dtype)], axis=1)
    else:
        pattern = jnp.concatenate([filters, jnp.zeros((group_count, tap_count + 1), filters.dtype)], axis=1)
    tiled = jnp.tile(pattern, (1, tap_count))[:, :2 * tap_count * tap_count]
    return tiled.reshape(group_count, tap_count, 2 * tap_count)

def causal_long(signal, row_ids, band, block_count):
    group_count, tap_count = (band.shape[0], band.shape[1])
    channels = signal.shape[1]

    def one_block(index):
        offset = index * tap_count
        window = lax.dynamic_slice_in_dim(signal, offset, 2 * tap_count, 0)
        window_ids = lax.dynamic_slice_in_dim(row_ids, offset, 2 * tap_count, 0)
        same = (window_ids[tap_count:][:, None] == window_ids[None, :]).astype(jnp.float32)
        weights = band.astype(jnp.float32) * same[None]
        grouped = window.reshape(2 * tap_count, group_count, channels // group_count).astype(jnp.float32)
        result = jnp.einsum('gij,jgc->igc', weights, grouped)
        return result.reshape(tap_count, channels)
    blocks = lax.map(one_block, jnp.arange(block_count, dtype=jnp.int32))
    return blocks.reshape(block_count * tap_count, channels)

def anti_long(signal, row_ids, band, block_count):
    group_count, tap_count = (band.shape[0], band.shape[1])
    channels = signal.shape[1]

    def one_block(index):
        offset = index * tap_count
        window = lax.dynamic_slice_in_dim(signal, offset, 2 * tap_count, 0)
        window_ids = lax.dynamic_slice_in_dim(row_ids, offset, 2 * tap_count, 0)
        same = (window_ids[:tap_count][:, None] == window_ids[None, :]).astype(jnp.float32)
        weights = band.astype(jnp.float32) * same[None]
        grouped = window.reshape(2 * tap_count, group_count, channels // group_count).astype(jnp.float32)
        result = jnp.einsum('gij,jgc->igc', weights, grouped)
        return result.reshape(tap_count, channels)
    blocks = lax.map(one_block, jnp.arange(block_count, dtype=jnp.int32))
    return blocks.reshape(block_count * tap_count, channels)

def tap_sums(grads, signal, row_ids, block_count, group_count, tap_count):
    channels = grads.shape[1]

    def one_block(carry, index):
        offset = index * tap_count
        rows_here = lax.dynamic_slice_in_dim(grads, offset, tap_count, 0).reshape(tap_count, group_count, channels // group_count).astype(jnp.float32)
        window = lax.dynamic_slice_in_dim(signal, offset, 2 * tap_count, 0).reshape(2 * tap_count, group_count, channels // group_count).astype(jnp.float32)
        window_ids = lax.dynamic_slice_in_dim(row_ids, offset, 2 * tap_count, 0)
        same = (window_ids[tap_count:][:, None] == window_ids[None, :]).astype(jnp.float32)
        products = jnp.einsum('igc,jgc->gij', rows_here, window) * same[None]
        flipped = products[:, :, ::-1].reshape(group_count, 2 * tap_count * tap_count)
        skewed = flipped[:, tap_count - 1:tap_count - 1 + tap_count * (2 * tap_count - 1)]
        skewed = skewed.reshape(group_count, tap_count, 2 * tap_count - 1)[:, :, :tap_count]
        return (carry + lax.optimization_barrier(jnp.sum(skewed, axis=1)), None)
    start = jnp.zeros((group_count, tap_count), jnp.float32)
    total, unused = lax.scan(one_block, start, jnp.arange(block_count, dtype=jnp.int32))
    return total

def short_causal(source, row_ids, weights, out_rows):
    width = weights.shape[0]
    lead = width - 1
    out_ids = row_ids[lead:lead + out_rows]
    total = jnp.zeros((out_rows, source.shape[1]), jnp.float32)
    for offset in range(width):
        begin = lead - offset
        piece = source[begin:begin + out_rows].astype(jnp.float32)
        same = (out_ids == row_ids[begin:begin + out_rows]).astype(jnp.float32)
        total = total + weights[offset][None, :] * piece * same[:, None]
    return total

def short_anti(grads, row_ids, weights, out_rows):
    width = weights.shape[0]
    out_ids = row_ids[:out_rows]
    total = jnp.zeros((out_rows, grads.shape[1]), jnp.float32)
    for offset in range(width):
        piece = grads[offset:offset + out_rows]
        same = (out_ids == row_ids[offset:offset + out_rows]).astype(jnp.float32)
        total = total + weights[offset][None, :] * piece * same[:, None]
    return total

def short_grad(grads, source, row_ids):
    out_rows = grads.shape[0]
    width = source.shape[0] - out_rows + 1
    lead = width - 1
    out_ids = row_ids[lead:lead + out_rows]
    sums = []
    for offset in range(width):
        begin = lead - offset
        piece = source[begin:begin + out_rows].astype(jnp.float32)
        same = (out_ids == row_ids[begin:begin + out_rows]).astype(jnp.float32)
        sums.append(lax.optimization_barrier(jnp.sum(grads * piece * same[:, None], axis=0)))
    return jnp.stack(sums)

def reference(q_in, k_in, v_in, grad_out, genome_ids, long_filter, short_filter):
    lead = SHORT - 1
    reach = TAPS + lead
    block_count = LEN // TAPS
    forward_band = toeplitz_band(long_filter, True)
    backward_band = toeplitz_band(long_filter, False)

    def one_sequence(items):
        query_rows, key_rows, value_rows, upstream, id_row = items
        ids_float = (id_row + 1).astype(jnp.float32)
        ids_back = jnp.concatenate([jnp.zeros((reach,), jnp.float32), ids_float])
        blank = jnp.zeros((reach, CH), jnp.bfloat16)
        key_ext = jnp.concatenate([blank, key_rows])
        value_ext = jnp.concatenate([blank, value_rows])
        query_ext = jnp.concatenate([blank[:lead], query_rows])
        query_ids = ids_back[reach - lead:]
        long_ids = ids_back[lead:]
        key_conv = short_causal(key_ext, ids_back, short_filter[1], LEN + TAPS)
        value_conv = short_causal(value_ext, ids_back, short_filter[2], LEN + TAPS)
        mixed = (key_conv * value_conv).astype(jnp.bfloat16)
        query_conv = short_causal(query_ext, query_ids, short_filter[0], LEN)
        filtered = causal_long(mixed, long_ids, forward_band, block_count)
        grad_filtered = (upstream.astype(jnp.float32) * query_conv).astype(jnp.bfloat16)
        grad_query = upstream.astype(jnp.float32) * filtered
        ids_front = jnp.concatenate([ids_float, jnp.zeros((TAPS,), jnp.float32)])
        grad_mixed = anti_long(jnp.concatenate([grad_filtered, jnp.zeros((TAPS, CH), jnp.bfloat16)]), ids_front, backward_band, block_count)
        grad_key = grad_mixed * value_conv[TAPS:]
        grad_value = grad_mixed * key_conv[TAPS:]
        short_ids = ids_front[:LEN + lead]
        edge = jnp.zeros((lead, CH), jnp.float32)
        out_q = short_anti(jnp.concatenate([grad_query, edge]), short_ids, short_filter[0], LEN).astype(jnp.bfloat16)
        out_k = short_anti(jnp.concatenate([grad_key, edge]), short_ids, short_filter[1], LEN).astype(jnp.bfloat16)
        out_v = short_anti(jnp.concatenate([grad_value, edge]), short_ids, short_filter[2], LEN).astype(jnp.bfloat16)
        long_part = tap_sums(grad_filtered, mixed, long_ids, block_count, GROUPS, TAPS)
        short_part = jnp.stack([short_grad(grad_query, query_ext, query_ids), short_grad(grad_key, key_ext[reach - lead:], query_ids), short_grad(grad_value, value_ext[reach - lead:], query_ids)])
        return (out_q, out_k, out_v, long_part, short_part)
    results = lax.map(one_sequence, (q_in, k_in, v_in, grad_out, genome_ids))
    grad_long = lax.optimization_barrier(jnp.sum(results[3], axis=0)) / math.sqrt(SEQS * LEN * GROUP)
    grad_short = lax.optimization_barrier(jnp.sum(results[4], axis=0)) / math.sqrt(SEQS * LEN)
    return (results[0], results[1], results[2], grad_long, grad_short)
```

```python
import functools
import math

import jax
import jax.numpy as jnp
from jax import lax
from jax.experimental import pallas as pl
from jax.experimental.pallas import tpu as pltpu
from jax.sharding import PartitionSpec as P

TAPS = 128
SHORT = 7
LANES = 128
PAD = 8
TAIL = 16
F32 = jnp.float32
BF16 = jnp.bfloat16
MESH = pl.DeviceIdType.MESH

TAILS, IDS_DOWN, IDS_UP, U_HALO, DZ_HALO, HEADS, FIRST_FREE = 0, 3, 4, 5, 6, 7, 8


def kernel(
    dims,
    q_ref, k_ref, v_ref, g_ref, ids_ref, lf_ref, sf_ref,
    oq_ref, ok_ref, ov_ref, ogl_ref, ogs_ref,
    x32, ks_ref, vs_ref, u_ref, dz_ref, uh_ref, dzh_ref, tails_ref, idp_ref, idn_ref,
    lfs_ref, h_ref, hr_ref, bc_ref, ba_ref, mc_ref, ma_ref, maf_ref, idc_ref, ms_ref, mas_ref,
    d32, dh_ref, pay_ref, rs_ref, red_ref, fin_ref,
    ssem, rsem,
):
    C, F, remote = dims
    R = q_ref.shape[1]
    T = q_ref.shape[2] // LANES
    B = R // TAPS
    G, tapw = lf_ref.shape
    GT = G // T
    width = LANES // GT
    NT = pay_ref.shape[0]
    per = NT // C
    ctx = lax.axis_index("ctx") if remote else 0
    fs = lax.axis_index("fsdp") if remote else 0
    nxt = {"ctx": lax.rem(ctx + 1, C)}
    prv = {"ctx": lax.rem(ctx + C - 1, C)}
    fil0 = FIRST_FREE
    rs0 = fil0 + F
    red0 = rs0 + C
    ag0 = red0 + F

    def rcopy(src, dst, slot, device):
        return pltpu.make_async_remote_copy(
            src_ref=src, dst_ref=dst, send_sem=ssem.at[slot], recv_sem=rsem.at[slot],
            device_id=device, device_id_type=MESH,
        )

    def ctx_peer(d):
        return lax.rem(ctx + d, C)

    def fs_peer(d):
        return lax.rem(fs + d, F)

    if remote:
        barrier = pltpu.get_barrier_semaphore()
        for d in range(1, C):
            pl.semaphore_signal(barrier, inc=1, device_id={"ctx": ctx_peer(d)}, device_id_type=MESH)
        for d in range(1, F):
            pl.semaphore_signal(barrier, inc=1, device_id={"fsdp": fs_peer(d)}, device_id_type=MESH)

    def fill_columns(row, chunk):
        idc_ref[chunk * LANES:(chunk + 1) * LANES, :] = jnp.transpose(
            jnp.broadcast_to(row, (LANES, LANES))
        )

    own_ids = ids_ref[...].astype(F32)
    for b in range(B):
        fill_columns(own_ids[:, b * LANES:(b + 1) * LANES], 1 + b)

    def fill_short_masks(r0, n):
        here = idc_ref[pl.ds(LANES + r0, n), :]
        for j in range(1, SHORT):
            back = idc_ref[pl.ds(LANES + r0 - j, n), :]
            ms_ref[j - 1, pl.ds(r0, n), :] = jnp.where(here == back, 1.0, 0.0)

    fill_short_masks(TAIL, R - TAIL)

    def lane_block(t):
        return pl.ds(pl.multiple_of(t * LANES, LANES), LANES)

    def widen(t, carry):
        for i, ref in enumerate((q_ref, k_ref, v_ref)):
            x32[i, t, PAD:PAD + R, :] = ref[0, :, lane_block(t)].astype(F32)
        return carry

    lax.fori_loop(0, T, widen, 0)

    if remote:
        pl.semaphore_wait(barrier, (C - 1) + (F - 1))
        tail_copies = [
            rcopy(ref.at[0, pl.ds(R - TAIL, TAIL), :], tails_ref.at[i], TAILS + i, nxt)
            for i, ref in enumerate((q_ref, k_ref, v_ref))
        ]
        ids_down = rcopy(ids_ref, idp_ref, IDS_DOWN, nxt)
        ids_up = rcopy(ids_ref, idn_ref, IDS_UP, prv)
        for copy in tail_copies + [ids_down, ids_up]:
            copy.start()
        filter_sends = [
            rcopy(lf_ref, lfs_ref.at[fs], fil0 + d, {"fsdp": fs_peer(d)}) for d in range(1, F)
        ]
        for copy in filter_sends:
            copy.start()
    lfs_ref[fs] = lf_ref[...]

    def short_rows(t, r0, n):
        convs = []
        for i in range(3):
            total = x32[i, t, pl.ds(PAD + r0, n), :] * sf_ref[i, 0:1, lane_block(t)]
            for j in range(1, SHORT):
                piece = x32[i, t, pl.ds(PAD + r0 - j, n), :] * ms_ref[j - 1, pl.ds(r0, n), :]
                total = total + piece * sf_ref[i, j:j + 1, lane_block(t)]
            convs.append(total)
        qs, ks, vs = convs
        ks_ref[t, pl.ds(r0, n), :] = ks
        vs_ref[t, pl.ds(r0, n), :] = vs
        u_ref[t, pl.ds(r0, n), :] = (ks * vs).astype(BF16)
        upstream = g_ref[0, pl.ds(r0, n), lane_block(t)].astype(F32)
        dz_ref[t, pl.ds(r0, n), :] = (upstream * qs).astype(BF16)

    def short_main(t, carry):
        short_rows(t, TAIL, R - TAIL)
        return carry

    lax.fori_loop(0, T, short_main, 0)

    if remote:
        u_copy = rcopy(u_ref.at[:, pl.ds(R - TAPS, TAPS), :], uh_ref, U_HALO, nxt)
        u_copy.start()
        for copy in tail_copies + [ids_down, ids_up]:
            copy.wait()

    prev_ids = idp_ref[...].astype(F32)[:, R - LANES:]
    next_ids = idn_ref[...].astype(F32)[:, :LANES]
    if remote:
        prev_ids = jnp.where(ctx == 0, -1.0, prev_ids)
        next_ids = jnp.where(ctx == C - 1, -1.0, next_ids)
    fill_columns(prev_ids, 0)
    fill_columns(next_ids, 1 + B)
    fill_short_masks(0, TAIL)

    def short_head(t, carry):
        for i in range(3):
            x32[i, t, 0:PAD, :] = tails_ref[i, :, lane_block(t)].astype(F32)[TAIL - PAD:]
        short_rows(t, 0, TAIL)
        return carry

    lax.fori_loop(0, T, short_head, 0)

    if remote:
        dz_copy = rcopy(dz_ref.at[:, pl.ds(0, TAPS), :], dzh_ref, DZ_HALO, prv)
        dz_copy.start()

    for j in range(1, SHORT):
        ahead = idc_ref[pl.ds(LANES + j, R), :]
        mas_ref[j - 1] = jnp.where(idc_ref[pl.ds(LANES, R), :] == ahead, 1.0, 0.0)
    rows = [prev_ids] + [own_ids[:, b * LANES:(b + 1) * LANES] for b in range(B)] + [next_ids]
    for b in range(B):
        column = idc_ref[(1 + b) * LANES:(2 + b) * LANES, :]
        for half in range(2):
            back = jnp.where(column == rows[b + half], 1.0, 0.0)
            ahead = jnp.where(column == rows[b + 1 + half], 1.0, 0.0)
            mc_ref[b, :, half * LANES:(half + 1) * LANES] = back.astype(BF16)
            ma_ref[b, :, half * LANES:(half + 1) * LANES] = ahead.astype(BF16)
            maf_ref[b, :, half * LANES:(half + 1) * LANES] = ahead

    if remote:
        for d in range(1, F):
            rcopy(lf_ref, lfs_ref.at[lax.rem(fs + F - d, F)], fil0 + d, {"fsdp": fs_peer(d)}).wait_recv()
    taps = jnp.zeros((G, TAPS), F32)
    flipped = jnp.zeros((G, TAPS), F32)
    place_row = lax.broadcasted_iota(jnp.int32, (tapw, TAPS), 0)
    place_col = lax.broadcasted_iota(jnp.int32, (tapw, TAPS), 1)
    for s in range(F):
        own = jnp.where(place_col == place_row + s * tapw, 1.0, 0.0).astype(BF16)
        turned = jnp.where(place_col == TAPS - 1 - s * tapw - place_row, 1.0, 0.0).astype(BF16)
        taps = taps + jnp.dot(lfs_ref[s], own, preferred_element_type=F32)
        flipped = flipped + jnp.dot(lfs_ref[s], turned, preferred_element_type=F32)
    h_ref[:, :TAPS] = taps
    h_ref[:, TAPS:] = jnp.zeros((G, TAPS), F32)
    hr_ref[:, :TAPS] = flipped
    hr_ref[:, TAPS:] = jnp.zeros((G, TAPS), F32)
    sub = lax.broadcasted_iota(jnp.int32, (8, 2 * TAPS), 0)

    def band_of(base, extra):
        for bit in (1, 2, 4):
            base = jnp.where((sub & bit) != 0, pltpu.roll(base, bit, 1), base)
        if extra:
            base = pltpu.roll(base, extra, 1)
        parts = [base] + [pltpu.roll(base, 8 * a, 1) for a in range(1, TAPS // 8)]
        return jnp.concatenate(parts, axis=0).astype(BF16)

    def build(g, carry):
        ba_ref[g] = band_of(jnp.broadcast_to(h_ref[pl.ds(g, 1), :], (8, 2 * TAPS)), 0)
        bc_ref[g] = band_of(jnp.broadcast_to(hr_ref[pl.ds(g, 1), :], (8, 2 * TAPS)), 1)
        return carry

    lax.fori_loop(0, G, build, 0)

    if remote:
        u_copy.wait()
        dz_copy.wait()
    lane_group = lax.broadcasted_iota(jnp.int32, (TAPS, LANES), 1) // width

    def dz_window(t, b):
        if b + 1 < B:
            return dz_ref[t, b * TAPS:(b + 2) * TAPS, :]
        return jnp.concatenate([dz_ref[t, b * TAPS:, :], dzh_ref[t]], axis=0)

    def u_window(t, b):
        if b > 0:
            return u_ref[t, (b - 1) * TAPS:(b + 1) * TAPS, :]
        return jnp.concatenate([uh_ref[t], u_ref[t, :TAPS, :]], axis=0)

    def banded(band_ref, mask, t, window):
        weights = band_ref[pl.ds(t * GT, GT)] * mask[None]
        product = jnp.dot(
            weights.reshape(GT * TAPS, 2 * TAPS), window, preferred_element_type=F32
        ).reshape(GT, TAPS, LANES)
        total = product[0]
        for g in range(1, GT):
            total = jnp.where(lane_group == g, product[g], total)
        return total

    def long_products(t, carry):
        for b in range(B):
            here = pl.ds(b * TAPS, TAPS)
            du = banded(ba_ref, ma_ref[b], t, dz_window(t, b))
            d32[1, t, here, :] = du * vs_ref[t, here, :]
            d32[2, t, here, :] = du * ks_ref[t, here, :]
            z = banded(bc_ref, mc_ref[b], t, u_window(t, b))
            d32[0, t, here, :] = g_ref[0, here, lane_block(t)].astype(F32) * z
        return carry

    lax.fori_loop(0, T, long_products, 0)
    if remote:
        heads = rcopy(d32.at[:, :, pl.ds(0, PAD), :], dh_ref, HEADS, prv)
        heads.start()

    long_scale = 1.0 / math.sqrt(dims_count(C, F, R) * width)
    short_scale = 1.0 / math.sqrt(dims_count(C, F, R))
    lane_row = lax.broadcasted_iota(jnp.int32, (1, LANES), 1) // width
    group_lanes = [jnp.where(lane_row == g, 1.0, 0.0).astype(BF16) for g in range(GT)]
    sub_all = lax.broadcasted_iota(jnp.int32, (GT * 8, 2 * TAPS), 0) & 7

    def long_grad(t, carry):
        sums = [None] * GT
        for b in range(B):
            signal = u_ref[t, b * TAPS:(b + 1) * TAPS, :]
            left = jnp.concatenate([signal * group_lanes[g] for g in range(GT)], axis=0)
            product = lax.dot_general(
                left, dz_window(t, b), (((1,), (1,)), ((), ())), preferred_element_type=F32
            )
            mask = maf_ref[b]
            for g in range(GT):
                part = product[g * TAPS:(g + 1) * TAPS] * mask
                sums[g] = part if sums[g] is None else sums[g] + part
        folded = []
        for g in range(GT):
            total = sums[g][0:8]
            for a in range(1, TAPS // 8):
                total = total + pltpu.roll(sums[g][8 * a:8 * a + 8], 2 * TAPS - 8 * a, 1)
            folded.append(total)
        stack = jnp.concatenate(folded, axis=0)
        for bit in (1, 2, 4):
            stack = jnp.where((sub_all & bit) != 0, pltpu.roll(stack, 2 * TAPS - bit, 1), stack)
        lags = jnp.sum(stack[:, :TAPS].reshape(GT, 8, TAPS), axis=1)
        pay_ref[3 * T + t] = lags * long_scale
        return carry

    lax.fori_loop(0, T, long_grad, 0)

    if remote:
        heads.wait()
    d32[:, :, R:R + PAD, :] = dh_ref[...]

    def short_grads(t, carry):
        for i in range(3):
            source = x32[i, t, PAD:PAD + R, :]
            sums = []
            for j in range(SHORT):
                term = d32[i, t, pl.ds(j, R), :] * source
                if j:
                    term = term * mas_ref[j - 1]
                sums.append(jnp.sum(term, axis=0, keepdims=True))
            sums.append(jnp.zeros((1, LANES), F32))
            pay_ref[i * T + t] = jnp.concatenate(sums, axis=0) * short_scale
        return carry

    lax.fori_loop(0, T, short_grads, 0)

    def own_slots(owner):
        return pl.ds(owner * per, per)

    if remote:
        scatter = [
            rcopy(pay_ref.at[own_slots(ctx_peer(d))], rs_ref.at[ctx], rs0 + d, {"ctx": ctx_peer(d)})
            for d in range(1, C)
        ]
        for copy in scatter:
            copy.start()
        rs_ref[ctx] = pay_ref[own_slots(ctx)]

    def outputs(i, o_ref):
        def one(t, carry):
            total = d32[i, t, pl.ds(0, R), :] * sf_ref[i, 0:1, lane_block(t)]
            for j in range(1, SHORT):
                piece = d32[i, t, pl.ds(j, R), :] * mas_ref[j - 1]
                total = total + piece * sf_ref[i, j:j + 1, lane_block(t)]
            o_ref[0, :, lane_block(t)] = total.astype(BF16)
            return carry

        lax.fori_loop(0, T, one, 0)

    outputs(0, oq_ref)
    if remote:
        for d in range(1, C):
            sender = lax.rem(ctx + C - d, C)
            rcopy(pay_ref.at[own_slots(ctx)], rs_ref.at[sender], rs0 + d, {"ctx": ctx_peer(d)}).wait_recv()
        total = rs_ref[0]
        for c in range(1, C):
            total = total + rs_ref[c]
        red_ref[fs] = total
        exchange = [
            rcopy(red_ref.at[fs], red_ref.at[fs], red0 + d, {"fsdp": fs_peer(d)}) for d in range(1, F)
        ]
        for copy in exchange:
            copy.start()
    outputs(1, ok_ref)
    if remote:
        for d in range(1, F):
            sender = lax.rem(fs + F - d, F)
            rcopy(red_ref.at[fs], red_ref.at[sender], red0 + d, {"fsdp": fs_peer(d)}).wait_recv()
        total = red_ref[0]
        for f in range(1, F):
            total = total + red_ref[f]
        fin_ref[own_slots(ctx)] = total
        gather = [
            rcopy(fin_ref.at[own_slots(ctx)], fin_ref.at[own_slots(ctx)], ag0 + d, {"ctx": ctx_peer(d)})
            for d in range(1, C)
        ]
        for copy in gather:
            copy.start()
    outputs(2, ov_ref)
    if remote:
        for d in range(1, C):
            sender = lax.rem(ctx + C - d, C)
            rcopy(
                fin_ref.at[own_slots(ctx)], fin_ref.at[own_slots(sender)], ag0 + d, {"ctx": ctx_peer(d)}
            ).wait_recv()
    for i in range(3):
        for t in range(T):
            ogs_ref[i, :, t * LANES:(t + 1) * LANES] = fin_ref[i * T + t, 0:SHORT, :]
    lags = fin_ref[3 * T:4 * T].reshape(G, TAPS)
    shift = lax.rem(TAPS - fs * tapw, TAPS)
    ogl_ref[...] = pltpu.roll(lags, shift, 1)[:, :tapw]
    if remote:
        for copy in filter_sends + scatter + exchange + gather:
            copy.wait_send()


def dims_count(contexts, sequences, rows):
    return contexts * sequences * rows


def mixer(C, F, remote, q_in, k_in, v_in, grad_out, ids, long_filter, short_filter):
    R, channels = q_in.shape[1], q_in.shape[2]
    T, B = channels // LANES, R // TAPS
    G, tapw = long_filter.shape
    NT = 4 * T
    per = NT // C
    wide = jax.ShapeDtypeStruct(q_in.shape, BF16)
    copies = FIRST_FREE + 2 * F + 2 * C
    vmem = pltpu.VMEM
    return pl.pallas_call(
        functools.partial(kernel, (C, F, remote)),
        out_shape=(
            wide, wide, wide,
            jax.ShapeDtypeStruct((G, tapw), F32),
            jax.ShapeDtypeStruct(short_filter.shape, F32),
        ),
        in_specs=[pl.BlockSpec(memory_space=vmem)] * 7,
        out_specs=[pl.BlockSpec(memory_space=vmem)] * 5,
        scratch_shapes=[
            vmem((3, T, PAD + R, LANES), F32),
            vmem((T, R, LANES), F32), vmem((T, R, LANES), F32),
            vmem((T, R, LANES), BF16), vmem((T, R, LANES), BF16),
            vmem((T, TAPS, LANES), BF16), vmem((T, TAPS, LANES), BF16),
            vmem((3, TAIL, channels), BF16),
            vmem((1, R), jnp.int32), vmem((1, R), jnp.int32),
            vmem((F, G, tapw), BF16),
            vmem((G, 2 * TAPS), F32), vmem((G, 2 * TAPS), F32),
            vmem((G, TAPS, 2 * TAPS), BF16), vmem((G, TAPS, 2 * TAPS), BF16),
            vmem((B, TAPS, 2 * TAPS), BF16), vmem((B, TAPS, 2 * TAPS), BF16),
            vmem((B, TAPS, 2 * TAPS), F32),
            vmem((R + 2 * LANES, LANES), F32),
            vmem((SHORT - 1, R, LANES), F32), vmem((SHORT - 1, R, LANES), F32),
            vmem((3, T, R + PAD, LANES), F32),
            vmem((3, T, PAD, LANES), F32),
            vmem((NT, 8, LANES), F32),
            vmem((C, per, 8, LANES), F32),
            vmem((F, per, 8, LANES), F32),
            vmem((NT, 8, LANES), F32),
            pltpu.SemaphoreType.DMA((copies,)),
            pltpu.SemaphoreType.DMA((copies,)),
        ],
        compiler_params=pltpu.CompilerParams(
            collective_id=0 if remote else None,
            has_side_effects=True,
            vmem_limit_bytes=60 * 1024 * 1024,
        ),
        name="mixer",
    )(q_in, k_in, v_in, grad_out, ids, long_filter, short_filter)


def solution(mesh):
    C, F = mesh.shape["ctx"], mesh.shape["fsdp"]
    wide = P("fsdp", "ctx", "tp")
    return jax.shard_map(
        functools.partial(mixer, C, F, True),
        mesh=mesh,
        in_specs=(wide, wide, wide, wide, P("fsdp", "ctx"), P("tp", "fsdp"), P(None, None, "tp")),
        out_specs=(wide, wide, wide, P("tp", "fsdp"), P(None, None, "tp")),
        check_vma=False,
    )
```

```python
import functools
import math

import jax
import jax.numpy as jnp
from jax import lax
from jax.experimental import pallas as pl
from jax.experimental.pallas import tpu as pltpu
from jax.sharding import PartitionSpec as P

TAPS = 128
SHORT = 7
LANES = 128
PAD = 8
TAIL = 16
CHUNK = 64
F32 = jnp.float32
BF16 = jnp.bfloat16
MESH = pl.DeviceIdType.MESH
NT_DIMS = (((1,), (1,)), ((), ()))

TAILS, IDS_DOWN, IDS_UP, U_HALO, DZ_HALO, HEADS, FIRST_FREE = 0, 3, 4, 5, 6, 7, 10


def kernel(
    dims,
    q_hbm, k_hbm, v_hbm, g_hbm, ids_hbm, lf_hbm, sf_hbm,
    oq_hbm, ok_hbm, ov_hbm, ogl_ref, ogs_ref,
    xin_ref, g_ref, ids_ref, lf_ref, sf_ref, out_ref,
    x32, pm_ref, ks_ref, vs_ref, u_ref, dz_ref, uh_ref, dzh_ref, ut_ref, dzt_ref,
    tails_ref, idp_ref, idn_ref,
    lfs_ref, h_ref, hn_ref, ba_ref, bc_ref, mc_ref, ma_ref, mq_ref, idc_ref, ms_ref, mas_ref,
    d32, dh_ref, gl_ref, turn_ref, pay_ref, rs_ref, red_ref, fin_ref,
    ssem, rsem, isem, osem,
):
    C, F, remote = dims
    R = xin_ref.shape[1]
    T = xin_ref.shape[2] // LANES
    B = R // TAPS
    tapw, G = lf_ref.shape
    GT = G // T
    width = LANES // GT
    per = 2 * T // C
    ctx = lax.axis_index("ctx") if remote else 0
    fs = lax.axis_index("fsdp") if remote else 0
    nxt = {"ctx": lax.rem(ctx + 1, C)}
    prv = {"ctx": lax.rem(ctx + C - 1, C)}
    fil0 = FIRST_FREE
    rs0 = fil0 + F
    red0 = rs0 + 2 * C
    ag0 = red0 + 2 * F

    def rcopy(src, dst, slot, device):
        return pltpu.make_async_remote_copy(
            src_ref=src, dst_ref=dst, send_sem=ssem.at[slot], recv_sem=rsem.at[slot],
            device_id=device, device_id_type=MESH,
        )

    def ctx_peer(d):
        return lax.rem(ctx + d, C)

    def fs_peer(d):
        return lax.rem(fs + d, F)

    if remote:
        barrier = pltpu.get_barrier_semaphore()
        for d in range(1, C):
            pl.semaphore_signal(barrier, inc=1, device_id={"ctx": ctx_peer(d)}, device_id_type=MESH)
        for d in range(1, F):
            pl.semaphore_signal(barrier, inc=1, device_id={"fsdp": fs_peer(d)}, device_id_type=MESH)

    loads = [
        pltpu.make_async_copy(src, dst, isem.at[n])
        for n, (src, dst) in enumerate((
            (ids_hbm, ids_ref), (q_hbm.at[0], xin_ref.at[0]), (k_hbm.at[0], xin_ref.at[1]),
            (v_hbm.at[0], xin_ref.at[2]), (sf_hbm, sf_ref), (g_hbm.at[0], g_ref), (lf_hbm, lf_ref),
        ))
    ]
    for load in loads:
        load.start()
    loads[0].wait()

    def fill_columns(row, chunk):
        idc_ref[chunk * LANES:(chunk + 1) * LANES, :] = jnp.transpose(
            jnp.broadcast_to(row, (LANES, LANES))
        )

    own_ids = ids_ref[...].astype(F32)
    for b in range(B):
        fill_columns(own_ids[:, b * LANES:(b + 1) * LANES], 1 + b)

    def fill_short_masks(r0, n):
        here = idc_ref[pl.ds(LANES + r0, n), :]
        for j in range(1, SHORT):
            back = idc_ref[pl.ds(LANES + r0 - j, n), :]
            ms_ref[j - 1, pl.ds(r0, n), :] = jnp.where(here == back, 1.0, 0.0)

    fill_short_masks(TAIL, R - TAIL)

    def lane_block(t):
        return pl.ds(pl.multiple_of(t * LANES, LANES), LANES)

    for load in loads[1:6]:
        load.wait()

    def widen(t, carry):
        for i in range(3):
            x32[i, t, PAD:PAD + R, :] = xin_ref[i, :, lane_block(t)].astype(F32)
        return carry

    def short_rows(t, r0, n):
        convs = []
        for i in range(3):
            total = x32[i, t, pl.ds(PAD + r0, n), :] * sf_ref[i, 0:1, lane_block(t)]
            for j in range(1, SHORT):
                piece = x32[i, t, pl.ds(PAD + r0 - j, n), :] * ms_ref[j - 1, pl.ds(r0, n), :]
                pm_ref[i, j - 1, t, pl.ds(r0, n), :] = piece
                total = total + piece * sf_ref[i, j:j + 1, lane_block(t)]
            convs.append(total)
        qs, ks, vs = convs
        ks_ref[t, pl.ds(r0, n), :] = ks
        vs_ref[t, pl.ds(r0, n), :] = vs
        u_ref[t, pl.ds(r0, n), :] = (ks * vs).astype(BF16)
        upstream = g_ref[pl.ds(r0, n), lane_block(t)].astype(F32)
        dz_ref[t, pl.ds(r0, n), :] = (upstream * qs).astype(BF16)

    def short_main(t, carry):
        widen(t, carry)
        short_rows(t, TAIL, CHUNK - TAIL)
        for r0 in range(CHUNK, R, CHUNK):
            short_rows(t, r0, CHUNK)
        return carry

    early = (T + 1) // 2
    lax.fori_loop(0, early, short_main, 0)

    loads[6].wait()
    if remote:
        pl.semaphore_wait(barrier, (C - 1) + (F - 1))
        filter_sends = [
            rcopy(lf_ref, lfs_ref.at[fs], fil0 + d, {"fsdp": fs_peer(d)}) for d in range(1, F)
        ]
        tail_copies = [
            rcopy(xin_ref.at[i, pl.ds(R - TAIL, TAIL), :], tails_ref.at[i], TAILS + i, nxt)
            for i in range(3)
        ]
        ids_down = rcopy(ids_ref, idp_ref, IDS_DOWN, nxt)
        ids_up = rcopy(ids_ref, idn_ref, IDS_UP, prv)
        for copy in filter_sends + [ids_down, ids_up] + tail_copies:
            copy.start()
    lfs_ref[fs] = lf_ref[...]
    lax.fori_loop(early, T, short_main, 0)

    if remote:
        u_copy = rcopy(u_ref.at[:, pl.ds(R - TAPS, TAPS), :], uh_ref, U_HALO, nxt)
        u_copy.start()
        for copy in tail_copies + [ids_down, ids_up]:
            copy.wait()

    prev_ids = idp_ref[...].astype(F32)[:, R - LANES:]
    next_ids = idn_ref[...].astype(F32)[:, :LANES]
    if remote:
        prev_ids = jnp.where(ctx == 0, -1.0, prev_ids)
        next_ids = jnp.where(ctx == C - 1, -1.0, next_ids)
    fill_columns(prev_ids, 0)
    fill_columns(next_ids, 1 + B)
    fill_short_masks(0, TAIL)

    def short_head(t, carry):
        for i in range(3):
            x32[i, t, 0:PAD, :] = tails_ref[i, :, lane_block(t)].astype(F32)[TAIL - PAD:]
        short_rows(t, 0, TAIL)
        return carry

    lax.fori_loop(0, T, short_head, 0)

    if remote:
        dz_copy = rcopy(dz_ref.at[:, pl.ds(0, TAPS), :], dzh_ref, DZ_HALO, prv)
        dz_copy.start()

    for j in range(1, SHORT):
        ahead = idc_ref[pl.ds(LANES + j, R), :]
        mas_ref[j - 1] = jnp.where(idc_ref[pl.ds(LANES, R), :] == ahead, 1.0, 0.0)
    rows = [prev_ids] + [own_ids[:, b * LANES:(b + 1) * LANES] for b in range(B)] + [next_ids]
    row_index = lax.broadcasted_iota(jnp.int32, (TAPS, LANES), 0)
    col_index = lax.broadcasted_iota(jnp.int32, (TAPS, LANES), 1)
    one = jnp.ones((TAPS, LANES), F32)
    zero = jnp.zeros((TAPS, LANES), F32)
    upper = jnp.where(col_index >= row_index, one, zero)
    above = jnp.where(col_index > row_index, one, zero)
    for b in range(B):
        column = idc_ref[(1 + b) * LANES:(2 + b) * LANES, :]
        same = [jnp.where(column == rows[b + n], one, zero) for n in range(3)]
        mc_ref[b, 0] = (same[0] * above).astype(BF16)
        mc_ref[b, 1] = (same[1] * (one - above)).astype(BF16)
        ma_ref[b, 0] = (same[1] * upper).astype(BF16)
        ma_ref[b, 1] = (same[2] * (one - upper)).astype(BF16)
        mq_ref[b] = same[1] * upper + same[2] * (one - upper)

    def dz_window(t, b):
        if b + 1 < B:
            return dz_ref[t, b * TAPS:(b + 2) * TAPS, :]
        return jnp.concatenate([dz_ref[t, b * TAPS:, :], dzh_ref[t]], axis=0)

    lane_row = lax.broadcasted_iota(jnp.int32, (1, LANES), 1) // width
    group_lanes = [jnp.where(lane_row == g, 1.0, 0.0).astype(BF16) for g in range(GT)]
    in_upper = col_index >= row_index

    def long_grad(t, b):
        signal = u_ref[t, b * TAPS:(b + 1) * TAPS, :]
        left = jnp.concatenate([signal * group_lanes[g] for g in range(GT)], axis=0)
        product = lax.dot_general(left, dz_window(t, b), NT_DIMS, preferred_element_type=F32)
        mask = mq_ref[b]
        folded = []
        for g in range(GT):
            part = product[g * TAPS:(g + 1) * TAPS]
            part = jnp.where(in_upper, part[:, :LANES], part[:, LANES:]) * mask
            total = part[0:8]
            for a in range(1, TAPS // 8):
                total = total + pltpu.roll(part[8 * a:8 * a + 8], LANES - 8 * a, 1)
            folded.append(total)
        return jnp.concatenate(folded, axis=0)

    def early_grad(t, carry):
        total = long_grad(t, 0)
        for b in range(1, B - 1):
            total = total + long_grad(t, b)
        gl_ref[t] = total
        return carry

    lax.fori_loop(0, T, early_grad, 0, unroll=2)

    def turn_own(t, carry):
        for b in range(B):
            ut_ref[t, 1 + b] = jnp.transpose(u_ref[t, b * TAPS:(b + 1) * TAPS, :])
            dzt_ref[t, b] = jnp.transpose(dz_ref[t, b * TAPS:(b + 1) * TAPS, :])
        return carry

    lax.fori_loop(0, T, turn_own, 0)

    if remote:
        for d in range(1, F):
            rcopy(lf_ref, lfs_ref.at[lax.rem(fs + F - d, F)], fil0 + d, {"fsdp": fs_peer(d)}).wait_recv()
    stacked = jnp.concatenate([lfs_ref[s] for s in range(F)], axis=0)
    unit_row = lax.broadcasted_iota(jnp.int32, (G, G), 0)
    unit_col = lax.broadcasted_iota(jnp.int32, (G, G), 1)
    unit = jnp.where(unit_row == unit_col, 1.0, 0.0).astype(BF16)
    taps = lax.dot_general(unit, stacked, NT_DIMS, preferred_element_type=F32)
    swap = jnp.where(((row_index + col_index) & (TAPS - 1)) == 0, 1.0, 0.0).astype(BF16)
    h_ref[...] = taps
    hn_ref[...] = jnp.dot(taps.astype(BF16), swap, preferred_element_type=F32)
    sub = lax.broadcasted_iota(jnp.int32, (8, TAPS), 0)
    unroll = 4

    def band_of(row):
        base = jnp.broadcast_to(row, (8, TAPS))
        for bit in (1, 2, 4):
            base = jnp.where((sub & bit) != 0, pltpu.roll(base, bit, 1), base)
        parts = [base] + [pltpu.roll(base, 8 * a, 1) for a in range(1, TAPS // 8)]
        return jnp.concatenate(parts, axis=0).astype(BF16)

    def build(n, carry):
        for m in range(unroll):
            g = n * unroll + m
            ba_ref[g] = band_of(h_ref[pl.ds(g, 1), :])
            bc_ref[g] = band_of(hn_ref[pl.ds(g, 1), :])
        return carry

    lax.fori_loop(0, G // unroll, build, 0)

    def banded(band_ref, mask_ref, b, t, left_ref, first):
        parts = []
        for g in range(GT):
            band = band_ref[t * GT + g]
            weights = jnp.concatenate([band * mask_ref[b, 0], band * mask_ref[b, 1]], axis=1)
            rows_g = slice(g * width, (g + 1) * width)
            left = jnp.concatenate([left_ref[t, first, rows_g, :], left_ref[t, first + 1, rows_g, :]], axis=1)
            parts.append(lax.dot_general(left, weights, NT_DIMS, preferred_element_type=F32))
        return jnp.transpose(jnp.concatenate(parts, axis=0))

    def backward_rows(t, b):
        here = pl.ds(b * TAPS, TAPS)
        du = banded(ba_ref, ma_ref, b, t, dzt_ref, b)
        d32[1, t, here, :] = du * vs_ref[t, here, :]
        d32[2, t, here, :] = du * ks_ref[t, here, :]

    def forward_rows(t, b):
        here = pl.ds(b * TAPS, TAPS)
        z = banded(bc_ref, mc_ref, b, t, ut_ref, b)
        d32[0, t, here, :] = g_ref[here, lane_block(t)].astype(F32) * z

    def inner_products(t, carry):
        for b in range(B - 1):
            backward_rows(t, b)
        for b in range(1, B):
            forward_rows(t, b)
        return carry

    lax.fori_loop(0, T, inner_products, 0, unroll=2)

    positions = C * F * R
    long_scale = 1.0 / math.sqrt(positions * width)
    short_scale = 1.0 / math.sqrt(positions)

    def short_grad(t, i):
        grads = d32[i, t, 0:R, :]
        sums = []
        for j in range(SHORT):
            source = pm_ref[i, j - 1, t] if j else x32[i, t, PAD:PAD + R, :]
            sums.append(jnp.sum(grads * source, axis=0, keepdims=True))
        sums.append(jnp.zeros((1, LANES), F32))
        return jnp.concatenate(sums, axis=0) * short_scale

    if remote:
        dz_copy.wait()

    def last_backward(t, carry):
        dzt_ref[t, B] = jnp.transpose(dzh_ref[t])
        backward_rows(t, B - 1)
        for i in (1, 2):
            pay_ref[0, (i - 1) * T + t] = short_grad(t, i)
        return carry

    lax.fori_loop(0, T, last_backward, 0, unroll=2)

    def heads(i):
        return rcopy(d32.at[i, :, pl.ds(0, PAD), :], dh_ref.at[i], HEADS + i, prv)

    def own_slots(owner):
        return pl.ds(owner * per, per)

    def scatter(n):
        return [
            rcopy(
                pay_ref.at[n, own_slots(ctx_peer(d))], rs_ref.at[n, ctx], rs0 + n * C + d,
                {"ctx": ctx_peer(d)},
            )
            for d in range(1, C)
        ]

    sends = []
    if remote:
        for copy in [heads(1), heads(2)] + scatter(0):
            copy.start()
        u_copy.wait()

    sub_all = lax.broadcasted_iota(jnp.int32, (GT * 8, TAPS), 0) & 7

    def last_forward(t, carry):
        ut_ref[t, 0] = jnp.transpose(uh_ref[t])
        forward_rows(t, 0)
        pay_ref[1, t] = short_grad(t, 0)
        return carry

    lax.fori_loop(0, T, last_forward, 0, unroll=2)
    if remote:
        heads(0).start()

    def late_grad(t, carry):
        stack = long_grad(t, B - 1)
        if B > 1:
            stack = stack + gl_ref[t]
        for bit in (1, 2, 4):
            stack = jnp.where((sub_all & bit) != 0, pltpu.roll(stack, LANES - bit, 1), stack)
        pay_ref[1, T + t] = jnp.sum(stack.reshape(GT, 8, TAPS), axis=1) * long_scale
        return carry

    lax.fori_loop(0, T, late_grad, 0, unroll=2)
    if remote:
        for copy in scatter(1):
            copy.start()
        for n in range(2):
            rs_ref[n, ctx] = pay_ref[n, own_slots(ctx)]

    def outputs(i, o_hbm):
        if remote:
            heads(i).wait_recv()
        d32[i, :, R:R + PAD, :] = dh_ref[i]

        def one_block(t, carry):
            total = d32[i, t, pl.ds(0, R), :] * sf_ref[i, 0:1, lane_block(t)]
            for j in range(1, SHORT):
                piece = d32[i, t, pl.ds(j, R), :] * mas_ref[j - 1]
                total = total + piece * sf_ref[i, j:j + 1, lane_block(t)]
            out_ref[i, :, lane_block(t)] = total.astype(BF16)
            return carry

        lax.fori_loop(0, T, one_block, 0)
        store = pltpu.make_async_copy(out_ref.at[i], o_hbm.at[0], osem.at[i])
        store.start()
        return store

    def exchange(n):
        return [
            rcopy(red_ref.at[n, fs], red_ref.at[n, fs], red0 + n * F + d, {"fsdp": fs_peer(d)})
            for d in range(1, F)
        ]

    def gather(n):
        own = fin_ref.at[n, own_slots(ctx)]
        return [rcopy(own, own, ag0 + n * C + d, {"ctx": ctx_peer(d)}) for d in range(1, C)]

    def sum_scattered(n):
        for d in range(1, C):
            sender = lax.rem(ctx + C - d, C)
            rcopy(
                pay_ref.at[n, own_slots(ctx)], rs_ref.at[n, sender], rs0 + n * C + d, {"ctx": ctx_peer(d)}
            ).wait_recv()
        total = rs_ref[n, 0]
        for c in range(1, C):
            total = total + rs_ref[n, c]
        red_ref[n, fs] = total
        for copy in exchange(n):
            copy.start()

    def sum_exchanged(n):
        for d in range(1, F):
            sender = lax.rem(fs + F - d, F)
            rcopy(
                red_ref.at[n, fs], red_ref.at[n, sender], red0 + n * F + d, {"fsdp": fs_peer(d)}
            ).wait_recv()
        total = red_ref[n, 0]
        for f in range(1, F):
            total = total + red_ref[n, f]
        fin_ref[n, own_slots(ctx)] = total
        for copy in gather(n):
            copy.start()

    def wait_gathered(n):
        for d in range(1, C):
            sender = lax.rem(ctx + C - d, C)
            rcopy(
                fin_ref.at[n, own_slots(ctx)], fin_ref.at[n, own_slots(sender)], ag0 + n * C + d,
                {"ctx": ctx_peer(d)},
            ).wait_recv()

    stores = [outputs(1, ok_hbm)]
    if remote:
        sum_scattered(0)
    stores.append(outputs(2, ov_hbm))
    if remote:
        sum_scattered(1)
    stores.append(outputs(0, oq_hbm))
    if remote:
        sum_exchanged(0)
        sum_exchanged(1)
        wait_gathered(0)
        wait_gathered(1)
    for t in range(T):
        lanes = slice(t * LANES, (t + 1) * LANES)
        ogs_ref[0, :, lanes] = fin_ref[1, t, 0:SHORT, :]
        ogs_ref[1, :, lanes] = fin_ref[0, t, 0:SHORT, :]
        ogs_ref[2, :, lanes] = fin_ref[0, T + t, 0:SHORT, :]
    lags = fin_ref[1, T:2 * T].reshape(G, TAPS)
    if G < LANES:
        lags = jnp.concatenate([lags, jnp.zeros((LANES - G, TAPS), F32)], axis=0)
    turn_ref[...] = jnp.transpose(lags)
    ogl_ref[...] = turn_ref[pl.ds(pl.multiple_of(fs * tapw, 8), tapw), :][:, :G]
    for store in stores:
        store.wait()
    if remote:
        for copy in filter_sends + [heads(i) for i in range(3)]:
            copy.wait_send()
        for n in range(2):
            for copy in scatter(n) + exchange(n) + gather(n):
                copy.wait_send()


def mixer(C, F, remote, q_in, k_in, v_in, grad_out, ids, long_filter, short_filter):
    R, channels = q_in.shape[1], q_in.shape[2]
    T, B = channels // LANES, R // TAPS
    G, tapw = long_filter.shape
    per = 2 * T // C
    wide = jax.ShapeDtypeStruct(q_in.shape, BF16)
    copies = FIRST_FREE + 3 * F + 4 * C
    vmem = pltpu.VMEM
    blocks = (T, TAPS, LANES)
    *grads, grad_long, grad_short = pl.pallas_call(
        functools.partial(kernel, (C, F, remote)),
        out_shape=(
            wide, wide, wide,
            jax.ShapeDtypeStruct((tapw, G), F32),
            jax.ShapeDtypeStruct(short_filter.shape, F32),
        ),
        in_specs=[pl.BlockSpec(memory_space=pl.ANY)] * 7,
        out_specs=[pl.BlockSpec(memory_space=pl.ANY)] * 3 + [pl.BlockSpec(memory_space=vmem)] * 2,
        scratch_shapes=[
            vmem((3, R, channels), BF16), vmem((R, channels), BF16),
            vmem((1, R), jnp.int32), vmem((tapw, G), BF16), vmem(short_filter.shape, F32),
            vmem((3, R, channels), BF16),
            vmem((3, T, PAD + R, LANES), F32),
            vmem((3, SHORT - 1, T, R, LANES), F32),
            vmem((T, R, LANES), F32), vmem((T, R, LANES), F32),
            vmem((T, R, LANES), BF16), vmem((T, R, LANES), BF16),
            vmem(blocks, BF16), vmem(blocks, BF16),
            vmem((T, B + 1, LANES, TAPS), BF16), vmem((T, B + 1, LANES, TAPS), BF16),
            vmem((3, TAIL, channels), BF16),
            vmem((1, R), jnp.int32), vmem((1, R), jnp.int32),
            vmem((F, tapw, G), BF16),
            vmem((G, TAPS), F32), vmem((G, TAPS), F32),
            vmem((G, TAPS, TAPS), BF16), vmem((G, TAPS, TAPS), BF16),
            vmem((B, 2, TAPS, LANES), BF16), vmem((B, 2, TAPS, LANES), BF16),
            vmem((B, TAPS, LANES), F32),
            vmem((R + 2 * LANES, LANES), F32),
            vmem((SHORT - 1, R, LANES), F32), vmem((SHORT - 1, R, LANES), F32),
            vmem((3, T, R + PAD, LANES), F32),
            vmem((3, T, PAD, LANES), F32),
            vmem((T, G // T * 8, LANES), F32),
            vmem((TAPS, LANES), F32),
            vmem((2, 2 * T, 8, LANES), F32),
            vmem((2, C, per, 8, LANES), F32),
            vmem((2, F, per, 8, LANES), F32),
            vmem((2, 2 * T, 8, LANES), F32),
            pltpu.SemaphoreType.DMA((copies,)),
            pltpu.SemaphoreType.DMA((copies,)),
            pltpu.SemaphoreType.DMA((7,)),
            pltpu.SemaphoreType.DMA((3,)),
        ],
        compiler_params=pltpu.CompilerParams(
            collective_id=0 if remote else None,
            has_side_effects=True,
            vmem_limit_bytes=60 * 1024 * 1024,
        ),
        name="mixer",
    )(q_in, k_in, v_in, grad_out, ids, long_filter.T, short_filter)
    return (*grads, grad_long.T, grad_short)


def solution(mesh):
    C, F = mesh.shape["ctx"], mesh.shape["fsdp"]
    wide = P("fsdp", "ctx", "tp")
    return jax.shard_map(
        functools.partial(mixer, C, F, True),
        mesh=mesh,
        in_specs=(wide, wide, wide, wide, P("fsdp", "ctx"), P("tp", "fsdp"), P(None, None, "tp")),
        out_specs=(wide, wide, wide, P("tp", "fsdp"), P(None, None, "tp")),
        check_vma=False,
    )
```

```python
import functools
import math

import jax
import jax.numpy as jnp
from jax import lax
from jax.experimental import pallas as pl
from jax.experimental.pallas import tpu as pltpu
from jax.sharding import PartitionSpec as P

TAPS = 128
SHORT = 7
LANES = 128
PAD = 8
TAIL = 16
CHUNK = 32
F32 = jnp.float32
BF16 = jnp.bfloat16
MESH = pl.DeviceIdType.MESH
NT_DIMS = (((1,), (1,)), ((), ()))

TAILS, IDS_DOWN, IDS_UP, U_HALO, DZ_HALO, HEADS, FILTERS = 0, 3, 4, 5, 6, 7, 10
SCATTER, EXCHANGE, GATHER, SLOTS = 11, 14, 17, 20
STREAMS = 3


def kernel(
    dims,
    q_hbm, k_hbm, v_hbm, g_hbm, ids_hbm, lf_hbm, sf_hbm,
    oq_hbm, ok_hbm, ov_hbm, ogl_ref, ogs_ref,
    xin_ref, g_ref, ids_ref, lf_ref, sf_ref, out_ref,
    x32, pm_ref, ks_ref, vs_ref, u_ref, dz_ref, uh_ref, dzh_ref, ut_ref, dzt_ref,
    tails_ref, idp_ref, idn_ref,
    lfs_ref, h_ref, hn_ref, ba_ref, bc_ref, mc_ref, ma_ref, mq_ref, idc_ref, ms_ref, mas_ref,
    d32, dh_ref, gl_ref, turn_ref, turned_ref, *rest,
):
    pay_refs, rs_refs, red_refs, fin_refs = (rest[n * STREAMS:(n + 1) * STREAMS] for n in range(4))
    ssem, rsem, isem, osem = rest[4 * STREAMS:]
    C, F, remote = dims
    R = xin_ref.shape[1]
    T = xin_ref.shape[2] // LANES
    B = R // TAPS
    tapw, G = lf_ref.shape
    GT = G // T
    width = LANES // GT
    per = 2 * T // C
    ctx = lax.axis_index("ctx") if remote else 0
    fs = lax.axis_index("fsdp") if remote else 0
    nxt = {"ctx": lax.rem(ctx + 1, C)}
    prv = {"ctx": lax.rem(ctx + C - 1, C)}
    ctx_order = sorted(range(1, C), key=lambda d: -min(d, C - d))
    fs_order = sorted(range(1, F), key=lambda d: (-min(d % (F // 2), F // 2 - d % (F // 2)) - 4 * (d * 2 >= F)))

    def rcopy(src, dst, slot, device):
        return pltpu.make_async_remote_copy(
            src_ref=src, dst_ref=dst, send_sem=ssem.at[slot], recv_sem=rsem.at[slot],
            device_id=device, device_id_type=MESH,
        )

    def whole(ref, slot):
        return rcopy(ref, ref, slot, prv)

    def ctx_peer(d):
        return lax.rem(ctx + d, C)

    def fs_peer(d):
        return lax.rem(fs + d, F)

    if remote:
        barrier = pltpu.get_barrier_semaphore()
        for d in fs_order:
            pl.semaphore_signal(barrier, inc=1, device_id={"fsdp": fs_peer(d)}, device_id_type=MESH)
        for d in ctx_order:
            pl.semaphore_signal(barrier, inc=1, device_id={"ctx": ctx_peer(d)}, device_id_type=MESH)

    loads = [
        pltpu.make_async_copy(src, dst, isem.at[n])
        for n, (src, dst) in enumerate((
            (ids_hbm, ids_ref), (q_hbm.at[0], xin_ref.at[0]), (k_hbm.at[0], xin_ref.at[1]),
            (v_hbm.at[0], xin_ref.at[2]), (sf_hbm, sf_ref), (g_hbm.at[0], g_ref), (lf_hbm, lf_ref),
        ))
    ]
    for load in loads:
        load.start()
    loads[0].wait()

    def fill_columns(row, chunk):
        idc_ref[chunk * LANES:(chunk + 1) * LANES, :] = jnp.transpose(
            jnp.broadcast_to(row, (LANES, LANES))
        )

    own_ids = ids_ref[...].astype(F32)
    for b in range(B):
        fill_columns(own_ids[:, b * LANES:(b + 1) * LANES], 1 + b)

    def fill_short_masks(r0, n):
        here = idc_ref[pl.ds(LANES + r0, n), :]
        for j in range(1, SHORT):
            back = idc_ref[pl.ds(LANES + r0 - j, n), :]
            ms_ref[j - 1, pl.ds(r0, n), :] = jnp.where(here == back, 1.0, 0.0)

    fill_short_masks(TAIL, R - TAIL)

    def lane_block(t):
        return pl.ds(pl.multiple_of(t * LANES, LANES), LANES)

    for load in loads[1:6]:
        load.wait()

    def widen(t, carry):
        for i in range(3):
            x32[i, t, PAD:PAD + R, :] = xin_ref[i, :, lane_block(t)].astype(F32)
        return carry

    def short_rows(t, r0, n):
        convs = []
        for i in range(3):
            total = x32[i, t, pl.ds(PAD + r0, n), :] * sf_ref[i, 0:1, lane_block(t)]
            for j in range(1, SHORT):
                piece = x32[i, t, pl.ds(PAD + r0 - j, n), :] * ms_ref[j - 1, pl.ds(r0, n), :]
                pm_ref[i, j - 1, t, pl.ds(r0, n), :] = piece
                total = total + piece * sf_ref[i, j:j + 1, lane_block(t)]
            convs.append(total)
        qs, ks, vs = convs
        ks_ref[t, pl.ds(r0, n), :] = ks
        vs_ref[t, pl.ds(r0, n), :] = vs
        u_ref[t, pl.ds(r0, n), :] = (ks * vs).astype(BF16)
        upstream = g_ref[pl.ds(r0, n), lane_block(t)].astype(F32)
        dz_ref[t, pl.ds(r0, n), :] = (upstream * qs).astype(BF16)

    def short_main(t, carry):
        widen(t, carry)
        short_rows(t, TAIL, CHUNK - TAIL)
        for r0 in range(CHUNK, R, CHUNK):
            short_rows(t, r0, CHUNK)
        return carry

    early = (T + 1) // 2
    lax.fori_loop(0, early, short_main, 0)

    loads[6].wait()
    if remote:
        pl.semaphore_wait(barrier, (C - 1) + (F - 1))
        filter_sends = [
            rcopy(lf_ref, lfs_ref.at[fs], FILTERS, {"fsdp": fs_peer(d)}) for d in fs_order
        ]
        tail_copies = [
            rcopy(xin_ref.at[i, pl.ds(R - TAIL, TAIL), :], tails_ref.at[i], TAILS + i, nxt)
            for i in range(3)
        ]
        ids_down = rcopy(ids_ref, idp_ref, IDS_DOWN, nxt)
        ids_up = rcopy(ids_ref, idn_ref, IDS_UP, prv)
        for copy in filter_sends + [ids_down, ids_up] + tail_copies:
            copy.start()
    lfs_ref[fs] = lf_ref[...]
    lax.fori_loop(early, T, short_main, 0)

    if remote:
        u_copy = rcopy(u_ref.at[:, pl.ds(R - TAPS, TAPS), :], uh_ref, U_HALO, nxt)
        u_copy.start()
        for copy in tail_copies + [ids_down, ids_up]:
            copy.wait()

    prev_ids = idp_ref[...].astype(F32)[:, R - LANES:]
    next_ids = idn_ref[...].astype(F32)[:, :LANES]
    if remote:
        prev_ids = jnp.where(ctx == 0, -1.0, prev_ids)
        next_ids = jnp.where(ctx == C - 1, -1.0, next_ids)
    fill_columns(prev_ids, 0)
    fill_columns(next_ids, 1 + B)
    fill_short_masks(0, TAIL)

    def short_head(t, carry):
        for i in range(3):
            x32[i, t, 0:PAD, :] = tails_ref[i, :, lane_block(t)].astype(F32)[TAIL - PAD:]
        short_rows(t, 0, TAIL)
        return carry

    lax.fori_loop(0, T, short_head, 0)

    if remote:
        dz_copy = rcopy(dz_ref.at[:, pl.ds(0, TAPS), :], dzh_ref, DZ_HALO, prv)
        dz_copy.start()

    for j in range(1, SHORT):
        ahead = idc_ref[pl.ds(LANES + j, R), :]
        mas_ref[j - 1] = jnp.where(idc_ref[pl.ds(LANES, R), :] == ahead, 1.0, 0.0)
    rows = [prev_ids] + [own_ids[:, b * LANES:(b + 1) * LANES] for b in range(B)] + [next_ids]
    row_index = lax.broadcasted_iota(jnp.int32, (TAPS, LANES), 0)
    col_index = lax.broadcasted_iota(jnp.int32, (TAPS, LANES), 1)
    one = jnp.ones((TAPS, LANES), F32)
    zero = jnp.zeros((TAPS, LANES), F32)
    upper = jnp.where(col_index >= row_index, one, zero)
    above = jnp.where(col_index > row_index, one, zero)
    for b in range(B):
        column = idc_ref[(1 + b) * LANES:(2 + b) * LANES, :]
        same = [jnp.where(column == rows[b + n], one, zero) for n in range(3)]
        mc_ref[b, 0] = (same[0] * above).astype(BF16)
        mc_ref[b, 1] = (same[1] * (one - above)).astype(BF16)
        ma_ref[b, 0] = (same[1] * upper).astype(BF16)
        ma_ref[b, 1] = (same[2] * (one - upper)).astype(BF16)
        mq_ref[b] = same[1] * upper + same[2] * (one - upper)

    def dz_window(t, b):
        if b + 1 < B:
            return dz_ref[t, b * TAPS:(b + 2) * TAPS, :]
        return jnp.concatenate([dz_ref[t, b * TAPS:, :], dzh_ref[t]], axis=0)

    lane_row = lax.broadcasted_iota(jnp.int32, (1, LANES), 1) // width
    group_lanes = [jnp.where(lane_row == g, 1.0, 0.0).astype(BF16) for g in range(GT)]
    in_upper = col_index >= row_index

    def long_grad(t, b):
        signal = u_ref[t, b * TAPS:(b + 1) * TAPS, :]
        left = jnp.concatenate([signal * group_lanes[g] for g in range(GT)], axis=0)
        product = lax.dot_general(left, dz_window(t, b), NT_DIMS, preferred_element_type=F32)
        mask = mq_ref[b]
        folded = []
        for g in range(GT):
            part = product[g * TAPS:(g + 1) * TAPS]
            part = jnp.where(in_upper, part[:, :LANES], part[:, LANES:]) * mask
            total = part[0:8]
            for a in range(1, TAPS // 8):
                total = total + pltpu.roll(part[8 * a:8 * a + 8], LANES - 8 * a, 1)
            folded.append(total)
        return jnp.concatenate(folded, axis=0)

    def early_grad(t, carry):
        total = long_grad(t, 0)
        for b in range(1, B - 1):
            total = total + long_grad(t, b)
        gl_ref[t] = total
        return carry

    lax.fori_loop(0, T, early_grad, 0, unroll=8)

    def turn_own(t, carry):
        for b in range(B):
            ut_ref[t, 1 + b] = jnp.transpose(u_ref[t, b * TAPS:(b + 1) * TAPS, :])
            dzt_ref[t, b] = jnp.transpose(dz_ref[t, b * TAPS:(b + 1) * TAPS, :])
        return carry

    lax.fori_loop(0, T, turn_own, 0, unroll=4)

    if remote:
        whole(lfs_ref.at[pl.ds(0, F - 1)], FILTERS).wait_recv()
    stacked = jnp.concatenate([lfs_ref[s] for s in range(F)], axis=0)
    unit_row = lax.broadcasted_iota(jnp.int32, (G, G), 0)
    unit_col = lax.broadcasted_iota(jnp.int32, (G, G), 1)
    unit = jnp.where(unit_row == unit_col, 1.0, 0.0).astype(BF16)
    taps = lax.dot_general(unit, stacked, NT_DIMS, preferred_element_type=F32)
    swap = jnp.where(((row_index + col_index) & (TAPS - 1)) == 0, 1.0, 0.0).astype(BF16)
    h_ref[...] = taps
    hn_ref[...] = jnp.dot(taps.astype(BF16), swap, preferred_element_type=F32)
    sub = lax.broadcasted_iota(jnp.int32, (8, TAPS), 0)
    unroll = 8

    def band_of(row):
        base = jnp.broadcast_to(row, (8, TAPS))
        for bit in (1, 2, 4):
            base = jnp.where((sub & bit) != 0, pltpu.roll(base, bit, 1), base)
        parts = [base] + [pltpu.roll(base, 8 * a, 1) for a in range(1, TAPS // 8)]
        return jnp.concatenate(parts, axis=0).astype(BF16)

    def build(n, carry):
        for m in range(unroll):
            g = n * unroll + m
            ba_ref[g] = band_of(h_ref[pl.ds(g, 1), :])
            bc_ref[g] = band_of(hn_ref[pl.ds(g, 1), :])
        return carry

    lax.fori_loop(0, G // unroll, build, 0)

    def banded(band_ref, mask_ref, b, t, left_ref, first):
        parts = []
        for g in range(GT):
            band = band_ref[t * GT + g]
            weights = jnp.concatenate([band * mask_ref[b, 0], band * mask_ref[b, 1]], axis=1)
            rows_g = slice(g * width, (g + 1) * width)
            left = jnp.concatenate([left_ref[t, first, rows_g, :], left_ref[t, first + 1, rows_g, :]], axis=1)
            parts.append(lax.dot_general(left, weights, NT_DIMS, preferred_element_type=F32))
        return jnp.transpose(jnp.concatenate(parts, axis=0))

    def backward_rows(t, b):
        here = pl.ds(b * TAPS, TAPS)
        du = banded(ba_ref, ma_ref, b, t, dzt_ref, b)
        d32[1, t, here, :] = du * vs_ref[t, here, :]
        d32[2, t, here, :] = du * ks_ref[t, here, :]

    def forward_rows(t, b):
        here = pl.ds(b * TAPS, TAPS)
        z = banded(bc_ref, mc_ref, b, t, ut_ref, b)
        d32[0, t, here, :] = g_ref[here, lane_block(t)].astype(F32) * z

    def inner_products(t, carry):
        for b in range(B - 1):
            backward_rows(t, b)
        for b in range(1, B):
            forward_rows(t, b)
        return carry

    lax.fori_loop(0, T, inner_products, 0, unroll=8)

    positions = C * F * R
    long_scale = 1.0 / math.sqrt(positions * width)
    short_scale = 1.0 / math.sqrt(positions)

    def short_grad(t, i):
        grads = d32[i, t, 0:R, :]
        sums = []
        for j in range(SHORT):
            source = pm_ref[i, j - 1, t] if j else x32[i, t, PAD:PAD + R, :]
            sums.append(jnp.sum(grads * source, axis=0, keepdims=True))
        sums.append(jnp.zeros((1, LANES), F32))
        return jnp.concatenate(sums, axis=0) * short_scale

    if remote:
        dz_copy.wait()

    def last_backward(t, carry):
        dzt_ref[t, B] = jnp.transpose(dzh_ref[t])
        backward_rows(t, B - 1)
        for i in (1, 2):
            pay_refs[0][(i - 1) * T + t] = short_grad(t, i)
        return carry

    lax.fori_loop(0, T, last_backward, 0, unroll=8)

    def heads(i):
        return rcopy(d32.at[i, :, pl.ds(0, PAD), :], dh_ref.at[i], HEADS + i, prv)

    def own_slots(owner):
        return pl.ds(owner * per, per)

    def scatter(n):
        for d in ctx_order:
            rcopy(
                pay_refs[n].at[own_slots(ctx_peer(d))], rs_refs[n].at[ctx], SCATTER + n,
                {"ctx": ctx_peer(d)},
            ).start()
        rs_refs[n][ctx] = pay_refs[n][own_slots(ctx)]

    if remote:
        scatter(0)
        heads(1).start()
        heads(2).start()

    sub_all = lax.broadcasted_iota(jnp.int32, (GT * 8, TAPS), 0) & 7

    def put_halves(ref, t, tile):
        ref[2 * t] = tile[0:4]
        ref[2 * t + 1] = tile[4:8]

    def late_grad(t, carry):
        stack = long_grad(t, B - 1)
        if B > 1:
            stack = stack + gl_ref[t]
        for bit in (1, 2, 4):
            stack = jnp.where((sub_all & bit) != 0, pltpu.roll(stack, LANES - bit, 1), stack)
        put_halves(pay_refs[1], t, jnp.sum(stack.reshape(GT, 8, TAPS), axis=1) * long_scale)
        return carry

    lax.fori_loop(0, T, late_grad, 0, unroll=8)
    if remote:
        scatter(1)
        u_copy.wait()

    def last_forward(t, carry):
        ut_ref[t, 0] = jnp.transpose(uh_ref[t])
        forward_rows(t, 0)
        put_halves(pay_refs[2], t, short_grad(t, 0))
        return carry

    lax.fori_loop(0, T, last_forward, 0, unroll=8)
    if remote:
        scatter(2)
        heads(0).start()

    def outputs(i, o_hbm):
        if remote:
            heads(i).wait_recv()
        d32[i, :, R:R + PAD, :] = dh_ref[i]

        def one_block(t, carry):
            total = d32[i, t, pl.ds(0, R), :] * sf_ref[i, 0:1, lane_block(t)]
            for j in range(1, SHORT):
                piece = d32[i, t, pl.ds(j, R), :] * mas_ref[j - 1]
                total = total + piece * sf_ref[i, j:j + 1, lane_block(t)]
            out_ref[i, :, lane_block(t)] = total.astype(BF16)
            return carry

        lax.fori_loop(0, T, one_block, 0)
        pltpu.make_async_copy(out_ref.at[i], o_hbm.at[0], osem.at[i]).start()

    def sum_scattered(n):
        whole(rs_refs[n].at[pl.ds(0, C - 1)], SCATTER + n).wait_recv()
        total = rs_refs[n][0]
        for c in range(1, C):
            total = total + rs_refs[n][c]
        own = red_refs[n].at[fs]
        own[...] = total
        for d in fs_order:
            rcopy(own, own, EXCHANGE + n, {"fsdp": fs_peer(d)}).start()

    def sum_exchanged(n):
        whole(red_refs[n].at[pl.ds(0, F - 1)], EXCHANGE + n).wait_recv()
        total = red_refs[n][0]
        for f in range(1, F):
            total = total + red_refs[n][f]
        own = fin_refs[n].at[own_slots(ctx)]
        own[...] = total
        for d in ctx_order:
            rcopy(own, own, GATHER + n, {"ctx": ctx_peer(d)}).start()

    def others(n):
        return fin_refs[n].at[pl.ds(0, (C - 1) * per)]

    outputs(1, ok_hbm)
    if remote:
        sum_scattered(0)
    outputs(2, ov_hbm)
    if remote:
        sum_scattered(1)
    outputs(0, oq_hbm)
    if remote:
        sum_scattered(2)
        for n in range(STREAMS):
            sum_exchanged(n)
        for n in range(STREAMS):
            whole(others(n), GATHER + n).wait_recv()
    for t in range(T):
        lanes = slice(t * LANES, (t + 1) * LANES)
        ogs_ref[0, 0:4, lanes] = fin_refs[2][2 * t]
        ogs_ref[0, 4:SHORT, lanes] = fin_refs[2][2 * t + 1, 0:SHORT - 4, :]
        ogs_ref[1, :, lanes] = fin_refs[0][t, 0:SHORT, :]
        ogs_ref[2, :, lanes] = fin_refs[0][T + t, 0:SHORT, :]
    if G < LANES:
        turn_ref[G:, :] = jnp.zeros((LANES - G, TAPS), F32)
    for n in range(2 * T):
        turn_ref[4 * n:4 * n + 4, :] = fin_refs[1][n]
    turned_ref[...] = jnp.transpose(turn_ref[...])
    ogl_ref[...] = turned_ref[pl.ds(pl.multiple_of(fs * tapw, 8), tapw), :][:, :G]
    for i, o_hbm in enumerate((oq_hbm, ok_hbm, ov_hbm)):
        pltpu.make_async_copy(out_ref.at[i], o_hbm.at[0], osem.at[i]).wait()
    if remote:
        whole(lfs_ref.at[pl.ds(0, F - 1)], FILTERS).wait_send()
        for i in range(3):
            heads(i).wait_send()
        for n in range(STREAMS):
            whole(rs_refs[n].at[pl.ds(0, C - 1)], SCATTER + n).wait_send()
            whole(red_refs[n].at[pl.ds(0, F - 1)], EXCHANGE + n).wait_send()
            whole(others(n), GATHER + n).wait_send()


def settle(*refs):
    count = (len(refs) - 2) // 3
    sources, targets, held = refs[:count], refs[count:2 * count], refs[2 * count:3 * count]
    in_sem, out_sem = refs[3 * count:]
    loads = [pltpu.make_async_copy(a, b, in_sem.at[n]) for n, (a, b) in enumerate(zip(sources, held))]
    stores = [pltpu.make_async_copy(a, b, out_sem.at[n]) for n, (a, b) in enumerate(zip(held, targets))]
    for load in loads:
        load.start()
    for load, store in zip(loads, stores):
        load.wait()
        store.start()
    for store in stores:
        store.wait()


def settled(arrays):
    anywhere = [pl.BlockSpec(memory_space=pl.ANY)] * len(arrays)
    shapes = [jax.ShapeDtypeStruct(a.shape, a.dtype) for a in arrays]
    return pl.pallas_call(
        settle,
        out_shape=shapes,
        in_specs=anywhere,
        out_specs=anywhere,
        scratch_shapes=[pltpu.VMEM(a.shape, a.dtype) for a in arrays]
        + [pltpu.SemaphoreType.DMA((len(arrays),))] * 2,
        compiler_params=pltpu.CompilerParams(vmem_limit_bytes=60 * 1024 * 1024),
        name="settle",
    )(*arrays)


def mixer(C, F, remote, q_in, k_in, v_in, grad_out, ids, long_filter, short_filter):
    R, channels = q_in.shape[1], q_in.shape[2]
    T, B = channels // LANES, R // TAPS
    G, tapw = long_filter.shape
    per = 2 * T // C
    wide = jax.ShapeDtypeStruct(q_in.shape, BF16)
    heights = (8, 4, 4)
    vmem = pltpu.VMEM
    blocks = (T, TAPS, LANES)
    results = pl.pallas_call(
        functools.partial(kernel, (C, F, remote)),
        out_shape=(
            wide, wide, wide,
            jax.ShapeDtypeStruct((tapw, G), F32),
            jax.ShapeDtypeStruct(short_filter.shape, F32),
        ),
        in_specs=[pl.BlockSpec(memory_space=pl.ANY)] * 7,
        out_specs=[pl.BlockSpec(memory_space=pl.ANY)] * 3 + [pl.BlockSpec(memory_space=vmem)] * 2,
        scratch_shapes=[
            vmem((3, R, channels), BF16), vmem((R, channels), BF16),
            vmem((1, R), jnp.int32), vmem((tapw, G), BF16), vmem(short_filter.shape, F32),
            vmem((3, R, channels), BF16),
            vmem((3, T, PAD + R, LANES), F32),
            vmem((3, SHORT - 1, T, R, LANES), F32),
            vmem((T, R, LANES), F32), vmem((T, R, LANES), F32),
            vmem((T, R, LANES), BF16), vmem((T, R, LANES), BF16),
            vmem(blocks, BF16), vmem(blocks, BF16),
            vmem((T, B + 1, LANES, TAPS), BF16), vmem((T, B + 1, LANES, TAPS), BF16),
            vmem((3, TAIL, channels), BF16),
            vmem((1, R), jnp.int32), vmem((1, R), jnp.int32),
            vmem((F, tapw, G), BF16),
            vmem((G, TAPS), F32), vmem((G, TAPS), F32),
            vmem((G, TAPS, TAPS), BF16), vmem((G, TAPS, TAPS), BF16),
            vmem((B, 2, TAPS, LANES), BF16), vmem((B, 2, TAPS, LANES), BF16),
            vmem((B, TAPS, LANES), F32),
            vmem((R + 2 * LANES, LANES), F32),
            vmem((SHORT - 1, R, LANES), F32), vmem((SHORT - 1, R, LANES), F32),
            vmem((3, T, R + PAD, LANES), F32),
            vmem((3, T, PAD, LANES), F32),
            vmem((T, G // T * 8, LANES), F32),
            vmem((TAPS, LANES), F32), vmem((TAPS, LANES), F32),
            *(vmem((2 * T, h, LANES), F32) for h in heights),
            *(vmem((C, per, h, LANES), F32) for h in heights),
            *(vmem((F, per, h, LANES), F32) for h in heights),
            *(vmem((2 * T, h, LANES), F32) for h in heights),
            pltpu.SemaphoreType.DMA((SLOTS,)),
            pltpu.SemaphoreType.DMA((SLOTS,)),
            pltpu.SemaphoreType.DMA((7,)),
            pltpu.SemaphoreType.DMA((3,)),
        ],
        compiler_params=pltpu.CompilerParams(
            collective_id=0 if remote else None,
            has_side_effects=True,
            vmem_limit_bytes=60 * 1024 * 1024,
        ),
        name="mixer",
    )(q_in, k_in, v_in, grad_out, ids, long_filter.T, short_filter)
    *grads, grad_long, grad_short = settled(results)
    return (*grads, grad_long.T, grad_short)


def solution(mesh):
    C, F = mesh.shape["ctx"], mesh.shape["fsdp"]
    wide = P("fsdp", "ctx", "tp")
    return jax.shard_map(
        functools.partial(mixer, C, F, True),
        mesh=mesh,
        in_specs=(wide, wide, wide, wide, P("fsdp", "ctx"), P("tp", "fsdp"), P(None, None, "tp")),
        out_specs=(wide, wide, wide, P("tp", "fsdp"), P(None, None, "tp")),
        check_vma=False,
    )
```

```python
import functools
import math

import jax
import jax.numpy as jnp
from jax import lax
from jax.experimental import pallas as pl
from jax.experimental.pallas import tpu as pltpu
from jax.sharding import PartitionSpec as P

TAPS = 128
SHORT = 7
LANES = 128
PAD = 8
TAIL = 16
CHUNK = 32
F32 = jnp.float32
BF16 = jnp.bfloat16
MESH = pl.DeviceIdType.MESH
NT_DIMS = (((1,), (1,)), ((), ()))

TAILS, IDS_DOWN, IDS_UP, U_HALO, DZ_HALO, HEADS, FILTERS = 0, 3, 4, 5, 6, 7, 10
SCATTER, EXCHANGE, GATHER, SLOTS = 11, 14, 17, 20
STREAMS = 3
CORES = 2


def kernel(
    dims,
    q_hbm, k_hbm, v_hbm, g_hbm, ids_hbm, lf_hbm, sf_hbm,
    oq_hbm, ok_hbm, ov_hbm, ogl_ref, ogs_ref,
    xin_ref, g_ref, ids_ref, lf_ref, sf_ref, out_ref,
    x32, pm_ref, ks_ref, vs_ref, u_ref, dz_ref, uh_ref, dzh_ref, ut_ref, dzt_ref,
    tails_ref, idp_ref, idn_ref,
    lfs_ref, h_ref, hn_ref, ba_ref, bc_ref, mc_ref, ma_ref, mq_ref, idc_ref, ms_ref, mas_ref,
    d32, dh_ref, gl_ref, turn_ref, turned_ref, *rest,
):
    pay_refs, rs_refs, red_refs, fin_refs = (rest[n * STREAMS:(n + 1) * STREAMS] for n in range(4))
    ssem, rsem, isem, osem = rest[4 * STREAMS:]
    C, F, remote = dims
    R = xin_ref.shape[1]
    T = xin_ref.shape[2] // LANES
    B = R // TAPS
    tapw, G = lf_ref.shape
    GT = G // T
    width = LANES // GT
    pers = [tiles // (min(4, F) * CORES) for tiles in (2 * T, T, T)]
    ctx = lax.axis_index("ctx") if remote else 0
    fs = lax.axis_index("fsdp") if remote else 0
    nxt = {"ctx": lax.rem(ctx + 1, C)}
    prv = {"ctx": lax.rem(ctx + C - 1, C)}
    XS = min(4, F)
    ZS, YS = F // XS, C // CORES
    z, x, y, core = fs // XS, fs % XS, ctx // CORES, ctx % CORES
    near_count, far_count = XS * CORES, ZS * YS
    near, far = x * CORES + core, z * YS + y
    ring = lambda d, n: min(d, n - d)
    fs_order = sorted(range(1, F), key=lambda d: -ring(d % XS, XS) - 4 * (d >= XS))
    near_order = sorted(range(1, near_count), key=lambda d: -ring(d, near_count))
    far_order = [(dz, dy) for dz in range(ZS) for dy in range(YS) if dz or dy]
    far_order.sort(key=lambda p: -ring(p[1], YS) - 4 * p[0])

    def rcopy(src, dst, slot, device):
        return pltpu.make_async_remote_copy(
            src_ref=src, dst_ref=dst, send_sem=ssem.at[slot], recv_sem=rsem.at[slot],
            device_id=device, device_id_type=MESH,
        )

    def whole(ref, slot):
        return rcopy(ref, ref, slot, prv)

    def near_peer(d):
        index = (near + d) % near_count
        return index, {"fsdp": z * XS + index // CORES, "ctx": y * CORES + index % CORES}

    def far_peer(dz, dy):
        return {"fsdp": (z + dz) % ZS * XS + x, "ctx": (y + dy) % YS * CORES + core}

    def fs_peer(d):
        return lax.rem(fs + d, F)

    if remote:
        barrier = pltpu.get_barrier_semaphore()
        for d in fs_order:
            pl.semaphore_signal(barrier, inc=1, device_id={"fsdp": fs_peer(d)}, device_id_type=MESH)
        greeted = [far_peer(dz, dy) for dz, dy in far_order if dy]
        greeted += [
            {"fsdp": z * XS + (x + dx) % XS, "ctx": y * CORES + 1 - core} for dx in range(XS)
        ]
        greeted.append({"ctx": (ctx + 2 * core - 1 + C) % C})
        for device in greeted:
            pl.semaphore_signal(barrier, inc=1, device_id=device, device_id_type=MESH)

    loads = [
        pltpu.make_async_copy(src, dst, isem.at[n])
        for n, (src, dst) in enumerate((
            (ids_hbm, ids_ref), (q_hbm.at[0], xin_ref.at[0]), (k_hbm.at[0], xin_ref.at[1]),
            (v_hbm.at[0], xin_ref.at[2]), (sf_hbm, sf_ref), (g_hbm.at[0], g_ref), (lf_hbm, lf_ref),
        ))
    ]
    for load in loads:
        load.start()
    loads[0].wait()

    def fill_columns(row, chunk):
        idc_ref[chunk * LANES:(chunk + 1) * LANES, :] = jnp.transpose(
            jnp.broadcast_to(row, (LANES, LANES))
        )

    own_ids = ids_ref[...].astype(F32)
    for b in range(B):
        fill_columns(own_ids[:, b * LANES:(b + 1) * LANES], 1 + b)

    def fill_short_masks(r0, n):
        here = idc_ref[pl.ds(LANES + r0, n), :]
        for j in range(1, SHORT):
            back = idc_ref[pl.ds(LANES + r0 - j, n), :]
            ms_ref[j - 1, pl.ds(r0, n), :] = jnp.where(here == back, 1.0, 0.0)

    fill_short_masks(TAIL, R - TAIL)

    def lane_block(t):
        return pl.ds(pl.multiple_of(t * LANES, LANES), LANES)

    for load in loads[1:6]:
        load.wait()

    def widen(t, carry):
        for i in range(3):
            x32[i, t, PAD:PAD + R, :] = xin_ref[i, :, lane_block(t)].astype(F32)
        return carry

    def short_rows(t, r0, n):
        convs = []
        for i in range(3):
            total = x32[i, t, pl.ds(PAD + r0, n), :] * sf_ref[i, 0:1, lane_block(t)]
            for j in range(1, SHORT):
                piece = x32[i, t, pl.ds(PAD + r0 - j, n), :] * ms_ref[j - 1, pl.ds(r0, n), :]
                pm_ref[i, j - 1, t, pl.ds(r0, n), :] = piece
                total = total + piece * sf_ref[i, j:j + 1, lane_block(t)]
            convs.append(total)
        qs, ks, vs = convs
        ks_ref[t, pl.ds(r0, n), :] = ks
        vs_ref[t, pl.ds(r0, n), :] = vs
        u_ref[t, pl.ds(r0, n), :] = (ks * vs).astype(BF16)
        upstream = g_ref[pl.ds(r0, n), lane_block(t)].astype(F32)
        dz_ref[t, pl.ds(r0, n), :] = (upstream * qs).astype(BF16)

    def short_main(t, carry):
        widen(t, carry)
        short_rows(t, TAIL, CHUNK - TAIL)
        for r0 in range(CHUNK, R, CHUNK):
            short_rows(t, r0, CHUNK)
        return carry

    early = (T + 1) // 2
    lax.fori_loop(0, early, short_main, 0)

    loads[6].wait()
    if remote:
        pl.semaphore_wait(barrier, len(greeted) + F - 1)
        filter_sends = [
            rcopy(lf_ref, lfs_ref.at[fs], FILTERS, {"fsdp": fs_peer(d)}) for d in fs_order
        ]
        tail_copies = [
            rcopy(xin_ref.at[i, pl.ds(R - TAIL, TAIL), :], tails_ref.at[i], TAILS + i, nxt)
            for i in range(3)
        ]
        ids_down = rcopy(ids_ref, idp_ref, IDS_DOWN, nxt)
        ids_up = rcopy(ids_ref, idn_ref, IDS_UP, prv)
        for copy in filter_sends + [ids_down, ids_up] + tail_copies:
            copy.start()
    lfs_ref[fs] = lf_ref[...]
    lax.fori_loop(early, T, short_main, 0)

    if remote:
        u_copy = rcopy(u_ref.at[:, pl.ds(R - TAPS, TAPS), :], uh_ref, U_HALO, nxt)
        u_copy.start()
        for copy in tail_copies + [ids_down, ids_up]:
            copy.wait()

    prev_ids = idp_ref[...].astype(F32)[:, R - LANES:]
    next_ids = idn_ref[...].astype(F32)[:, :LANES]
    if remote:
        prev_ids = jnp.where(ctx == 0, -1.0, prev_ids)
        next_ids = jnp.where(ctx == C - 1, -1.0, next_ids)
    fill_columns(prev_ids, 0)
    fill_columns(next_ids, 1 + B)
    fill_short_masks(0, TAIL)

    def short_head(t, carry):
        for i in range(3):
            x32[i, t, 0:PAD, :] = tails_ref[i, :, lane_block(t)].astype(F32)[TAIL - PAD:]
        short_rows(t, 0, TAIL)
        return carry

    lax.fori_loop(0, T, short_head, 0)

    if remote:
        dz_copy = rcopy(dz_ref.at[:, pl.ds(0, TAPS), :], dzh_ref, DZ_HALO, prv)
        dz_copy.start()

    for j in range(1, SHORT):
        ahead = idc_ref[pl.ds(LANES + j, R), :]
        mas_ref[j - 1] = jnp.where(idc_ref[pl.ds(LANES, R), :] == ahead, 1.0, 0.0)
    rows = [prev_ids] + [own_ids[:, b * LANES:(b + 1) * LANES] for b in range(B)] + [next_ids]
    row_index = lax.broadcasted_iota(jnp.int32, (TAPS, LANES), 0)
    col_index = lax.broadcasted_iota(jnp.int32, (TAPS, LANES), 1)
    one = jnp.ones((TAPS, LANES), F32)
    zero = jnp.zeros((TAPS, LANES), F32)
    upper = jnp.where(col_index >= row_index, one, zero)
    above = jnp.where(col_index > row_index, one, zero)
    for b in range(B):
        column = idc_ref[(1 + b) * LANES:(2 + b) * LANES, :]
        same = [jnp.where(column == rows[b + n], one, zero) for n in range(3)]
        mc_ref[b, :, :LANES] = (same[0] * above).astype(BF16)
        mc_ref[b, :, LANES:] = (same[1] * (one - above)).astype(BF16)
        ma_ref[b, :, :LANES] = (same[1] * upper).astype(BF16)
        ma_ref[b, :, LANES:] = (same[2] * (one - upper)).astype(BF16)
        mq_ref[b] = same[1] * upper + same[2] * (one - upper)

    def dz_window(t, b):
        if b + 1 < B:
            return dz_ref[t, b * TAPS:(b + 2) * TAPS, :]
        return jnp.concatenate([dz_ref[t, b * TAPS:, :], dzh_ref[t]], axis=0)

    lane_row = lax.broadcasted_iota(jnp.int32, (1, LANES), 1) // width
    group_lanes = [jnp.where(lane_row == g, 1.0, 0.0).astype(BF16) for g in range(GT)]
    in_upper = col_index >= row_index

    def long_grad(t, b):
        signal = u_ref[t, b * TAPS:(b + 1) * TAPS, :]
        left = jnp.concatenate([signal * group_lanes[g] for g in range(GT)], axis=0)
        product = lax.dot_general(left, dz_window(t, b), NT_DIMS, preferred_element_type=F32)
        mask = mq_ref[b]
        parts = []
        for g in range(GT):
            part = product[g * TAPS:(g + 1) * TAPS]
            parts.append(jnp.where(in_upper, part[:, :LANES], part[:, LANES:]) * mask)
        return parts

    def early_grad(t, carry):
        for b in range(B - 1):
            for g, part in enumerate(long_grad(t, b)):
                gl_ref[t * GT + g] = part if b == 0 else gl_ref[t * GT + g] + part
        return carry

    lax.fori_loop(0, T, early_grad, 0, unroll=8)

    def turn_own(t, carry):
        for b in range(B):
            ut_ref[t, 1 + b] = jnp.transpose(u_ref[t, b * TAPS:(b + 1) * TAPS, :])
            dzt_ref[t, b] = jnp.transpose(dz_ref[t, b * TAPS:(b + 1) * TAPS, :])
        return carry

    lax.fori_loop(0, T, turn_own, 0, unroll=4)

    if remote:
        whole(lfs_ref.at[pl.ds(0, F - 1)], FILTERS).wait_recv()
    stacked = jnp.concatenate([lfs_ref[s] for s in range(F)], axis=0)
    unit_row = lax.broadcasted_iota(jnp.int32, (G, G), 0)
    unit_col = lax.broadcasted_iota(jnp.int32, (G, G), 1)
    unit = jnp.where(unit_row == unit_col, 1.0, 0.0).astype(BF16)
    taps = lax.dot_general(unit, stacked, NT_DIMS, preferred_element_type=F32)
    swap = jnp.where(((row_index + col_index) & (TAPS - 1)) == 0, 1.0, 0.0).astype(BF16)
    h_ref[...] = taps
    hn_ref[...] = jnp.dot(taps.astype(BF16), swap, preferred_element_type=F32)
    sub = lax.broadcasted_iota(jnp.int32, (8, TAPS), 0)
    unroll = 8

    def band_of(row):
        base = jnp.broadcast_to(row, (8, TAPS))
        for bit in (1, 2, 4):
            base = jnp.where((sub & bit) != 0, pltpu.roll(base, bit, 1), base)
        parts = [base] + [pltpu.roll(base, 8 * a, 1) for a in range(1, TAPS // 8)]
        return jnp.concatenate(parts, axis=0).astype(BF16)

    def build(n, carry):
        for m in range(unroll):
            g = n * unroll + m
            for band_ref, row_ref in ((ba_ref, h_ref), (bc_ref, hn_ref)):
                band = band_of(row_ref[pl.ds(g, 1), :])
                band_ref[g] = jnp.concatenate([band, band], axis=1)
        return carry

    lax.fori_loop(0, G // unroll, build, 0)

    def banded(band_ref, mask_ref, b, t, left_ref, first):
        parts = []
        for g in range(GT):
            band = band_ref[t * GT + g]
            weights = band * mask_ref[b]
            rows_g = slice(g * width, (g + 1) * width)
            left = jnp.concatenate([left_ref[t, first, rows_g, :], left_ref[t, first + 1, rows_g, :]], axis=1)
            parts.append(lax.dot_general(left, weights, NT_DIMS, preferred_element_type=F32))
        return jnp.transpose(jnp.concatenate(parts, axis=0))

    def backward_rows(t, b):
        here = pl.ds(b * TAPS, TAPS)
        du = banded(ba_ref, ma_ref, b, t, dzt_ref, b)
        d32[1, t, here, :] = du * vs_ref[t, here, :]
        d32[2, t, here, :] = du * ks_ref[t, here, :]

    def forward_rows(t, b):
        here = pl.ds(b * TAPS, TAPS)
        z = banded(bc_ref, mc_ref, b, t, ut_ref, b)
        d32[0, t, here, :] = g_ref[here, lane_block(t)].astype(F32) * z

    def inner_products(t, carry):
        for b in range(B - 1):
            backward_rows(t, b)
        for b in range(1, B):
            forward_rows(t, b)
        return carry

    lax.fori_loop(0, T, inner_products, 0, unroll=8)

    positions = C * F * R
    long_scale = 1.0 / math.sqrt(positions * width)
    short_scale = 1.0 / math.sqrt(positions)

    def short_grad(t, i):
        grads = d32[i, t, 0:R, :]
        sums = []
        for j in range(SHORT):
            source = pm_ref[i, j - 1, t] if j else x32[i, t, PAD:PAD + R, :]
            sums.append(jnp.sum(grads * source, axis=0, keepdims=True))
        sums.append(jnp.zeros((1, LANES), F32))
        return jnp.concatenate(sums, axis=0) * short_scale

    if remote:
        dz_copy.wait()

    def last_backward(t, carry):
        dzt_ref[t, B] = jnp.transpose(dzh_ref[t])
        backward_rows(t, B - 1)
        for i in (1, 2):
            pay_refs[0][(i - 1) * T + t] = short_grad(t, i)
        return carry

    lax.fori_loop(0, T, last_backward, 0, unroll=8)

    def heads(i):
        return rcopy(d32.at[i, :, pl.ds(0, PAD), :], dh_ref.at[i], HEADS + i, prv)

    def own_slots(n, owner):
        return pl.ds(owner * pers[n], pers[n])

    def scatter(n):
        for d in near_order:
            index, device = near_peer(d)
            rcopy(pay_refs[n].at[own_slots(n, index)], rs_refs[n].at[near], SCATTER + n, device).start()
        rs_refs[n][near] = pay_refs[n][own_slots(n, near)]

    if remote:
        scatter(0)
        heads(1).start()
        heads(2).start()

    sub_all = lax.broadcasted_iota(jnp.int32, (GT * 8, TAPS), 0) & 7

    def late_grad(t, carry):
        folded = []
        for g, part in enumerate(long_grad(t, B - 1)):
            if B > 1:
                part = part + gl_ref[t * GT + g]
            total = part[0:8]
            for a in range(1, TAPS // 8):
                total = total + pltpu.roll(part[8 * a:8 * a + 8], LANES - 8 * a, 1)
            folded.append(total)
        stack = jnp.concatenate(folded, axis=0)
        for bit in (1, 2, 4):
            stack = jnp.where((sub_all & bit) != 0, pltpu.roll(stack, LANES - bit, 1), stack)
        pay_refs[1][t] = jnp.sum(stack.reshape(GT, 8, TAPS), axis=1) * long_scale
        return carry

    lax.fori_loop(0, T, late_grad, 0, unroll=8)
    if remote:
        scatter(1)
        u_copy.wait()

    def last_forward(t, carry):
        ut_ref[t, 0] = jnp.transpose(uh_ref[t])
        forward_rows(t, 0)
        pay_refs[2][t] = short_grad(t, 0)
        return carry

    lax.fori_loop(0, T, last_forward, 0, unroll=8)
    if remote:
        scatter(2)
        heads(0).start()

    def outputs(i, o_hbm):
        if remote:
            heads(i).wait_recv()
        d32[i, :, R:R + PAD, :] = dh_ref[i]

        def one_block(t, carry):
            total = d32[i, t, pl.ds(0, R), :] * sf_ref[i, 0:1, lane_block(t)]
            for j in range(1, SHORT):
                piece = d32[i, t, pl.ds(j, R), :] * mas_ref[j - 1]
                total = total + piece * sf_ref[i, j:j + 1, lane_block(t)]
            out_ref[i, :, lane_block(t)] = total.astype(BF16)
            return carry

        lax.fori_loop(0, T, one_block, 0)
        pltpu.make_async_copy(out_ref.at[i], o_hbm.at[0], osem.at[i]).start()

    def sum_scattered(n):
        whole(rs_refs[n].at[pl.ds(0, near_count - 1)], SCATTER + n).wait_recv()
        total = rs_refs[n][0]
        for c in range(1, near_count):
            total = total + rs_refs[n][c]
        own = red_refs[n].at[far]
        own[...] = total
        for dz, dy in far_order:
            rcopy(own, own, EXCHANGE + n, far_peer(dz, dy)).start()

    def sum_exchanged(n):
        whole(red_refs[n].at[pl.ds(0, far_count - 1)], EXCHANGE + n).wait_recv()
        total = red_refs[n][0]
        for f in range(1, far_count):
            total = total + red_refs[n][f]
        own = fin_refs[n].at[own_slots(n, near)]
        own[...] = total
        for d in near_order:
            rcopy(own, own, GATHER + n, near_peer(d)[1]).start()

    def others(n):
        return fin_refs[n].at[pl.ds(0, (near_count - 1) * pers[n])]

    outputs(1, ok_hbm)
    if remote:
        sum_scattered(0)
    outputs(2, ov_hbm)
    if remote:
        sum_scattered(1)
    outputs(0, oq_hbm)
    if remote:
        sum_scattered(2)
        for n in range(STREAMS):
            sum_exchanged(n)
        for n in range(STREAMS):
            whole(others(n), GATHER + n).wait_recv()
    for t in range(T):
        lanes = slice(t * LANES, (t + 1) * LANES)
        ogs_ref[0, :, lanes] = fin_refs[2][t, 0:SHORT, :]
        ogs_ref[1, :, lanes] = fin_refs[0][t, 0:SHORT, :]
        ogs_ref[2, :, lanes] = fin_refs[0][T + t, 0:SHORT, :]
    if G < LANES:
        turn_ref[G:, :] = jnp.zeros((LANES - G, TAPS), F32)
    for t in range(T):
        turn_ref[GT * t:GT * t + GT, :] = fin_refs[1][t]
    turned_ref[...] = jnp.transpose(turn_ref[...])
    ogl_ref[...] = turned_ref[pl.ds(pl.multiple_of(fs * tapw, 8), tapw), :][:, :G]
    for i, o_hbm in enumerate((oq_hbm, ok_hbm, ov_hbm)):
        pltpu.make_async_copy(out_ref.at[i], o_hbm.at[0], osem.at[i]).wait()
    if remote:
        whole(lfs_ref.at[pl.ds(0, F - 1)], FILTERS).wait_send()
        for i in range(3):
            heads(i).wait_send()
        for n in range(STREAMS):
            whole(rs_refs[n].at[pl.ds(0, near_count - 1)], SCATTER + n).wait_send()
            whole(red_refs[n].at[pl.ds(0, far_count - 1)], EXCHANGE + n).wait_send()
            whole(others(n), GATHER + n).wait_send()


def settle(*refs):
    count = (len(refs) - 2) // 3
    sources, targets, held = refs[:count], refs[count:2 * count], refs[2 * count:3 * count]
    in_sem, out_sem = refs[3 * count:]
    loads = [pltpu.make_async_copy(a, b, in_sem.at[n]) for n, (a, b) in enumerate(zip(sources, held))]
    stores = [pltpu.make_async_copy(a, b, out_sem.at[n]) for n, (a, b) in enumerate(zip(held, targets))]
    for load in loads:
        load.start()
    for load, store in zip(loads, stores):
        load.wait()
        store.start()
    for store in stores:
        store.wait()


def settled(arrays):
    anywhere = [pl.BlockSpec(memory_space=pl.ANY)] * len(arrays)
    shapes = [jax.ShapeDtypeStruct(a.shape, a.dtype) for a in arrays]
    return pl.pallas_call(
        settle,
        out_shape=shapes,
        in_specs=anywhere,
        out_specs=anywhere,
        scratch_shapes=[pltpu.VMEM(a.shape, a.dtype) for a in arrays]
        + [pltpu.SemaphoreType.DMA((len(arrays),))] * 2,
        compiler_params=pltpu.CompilerParams(vmem_limit_bytes=60 * 1024 * 1024),
        name="settle",
    )(*arrays)


def mixer(C, F, remote, q_in, k_in, v_in, grad_out, ids, long_filter, short_filter):
    R, channels = q_in.shape[1], q_in.shape[2]
    T, B = channels // LANES, R // TAPS
    G, tapw = long_filter.shape
    wide = jax.ShapeDtypeStruct(q_in.shape, BF16)
    streams = (2 * T, T, T)
    near = min(4, F) * CORES
    far = C * F // near
    vmem = pltpu.VMEM
    blocks = (T, TAPS, LANES)
    results = pl.pallas_call(
        functools.partial(kernel, (C, F, remote)),
        out_shape=(
            wide, wide, wide,
            jax.ShapeDtypeStruct((tapw, G), F32),
            jax.ShapeDtypeStruct(short_filter.shape, F32),
        ),
        in_specs=[pl.BlockSpec(memory_space=pl.ANY)] * 7,
        out_specs=[pl.BlockSpec(memory_space=pl.ANY)] * 3 + [pl.BlockSpec(memory_space=vmem)] * 2,
        scratch_shapes=[
            vmem((3, R, channels), BF16), vmem((R, channels), BF16),
            vmem((1, R), jnp.int32), vmem((tapw, G), BF16), vmem(short_filter.shape, F32),
            vmem((3, R, channels), BF16),
            vmem((3, T, PAD + R, LANES), F32),
            vmem((3, SHORT - 1, T, R, LANES), F32),
            vmem((T, R, LANES), F32), vmem((T, R, LANES), F32),
            vmem((T, R, LANES), BF16), vmem((T, R, LANES), BF16),
            vmem(blocks, BF16), vmem(blocks, BF16),
            vmem((T, B + 1, LANES, TAPS), BF16), vmem((T, B + 1, LANES, TAPS), BF16),
            vmem((3, TAIL, channels), BF16),
            vmem((1, R), jnp.int32), vmem((1, R), jnp.int32),
            vmem((F, tapw, G), BF16),
            vmem((G, TAPS), F32), vmem((G, TAPS), F32),
            vmem((G, TAPS, 2 * TAPS), BF16), vmem((G, TAPS, 2 * TAPS), BF16),
            vmem((B, TAPS, 2 * LANES), BF16), vmem((B, TAPS, 2 * LANES), BF16),
            vmem((B, TAPS, LANES), F32),
            vmem((R + 2 * LANES, LANES), F32),
            vmem((SHORT - 1, R, LANES), F32), vmem((SHORT - 1, R, LANES), F32),
            vmem((3, T, R + PAD, LANES), F32),
            vmem((3, T, PAD, LANES), F32),
            vmem((G, TAPS, LANES), F32),
            vmem((TAPS, LANES), F32), vmem((TAPS, LANES), F32),
            *(vmem((tiles, 8, LANES), F32) for tiles in streams),
            *(vmem((near, tiles // near, 8, LANES), F32) for tiles in streams),
            *(vmem((far, tiles // near, 8, LANES), F32) for tiles in streams),
            *(vmem((tiles, 8, LANES), F32) for tiles in streams),
            pltpu.SemaphoreType.DMA((SLOTS,)),
            pltpu.SemaphoreType.DMA((SLOTS,)),
            pltpu.SemaphoreType.DMA((7,)),
            pltpu.SemaphoreType.DMA((3,)),
        ],
        compiler_params=pltpu.CompilerParams(
            collective_id=0 if remote else None,
            has_side_effects=True,
            vmem_limit_bytes=60 * 1024 * 1024,
        ),
        name="mixer",
    )(q_in, k_in, v_in, grad_out, ids, long_filter.T, short_filter)
    *grads, grad_long, grad_short = settled(results)
    return (*grads, grad_long.T, grad_short)


def solution(mesh):
    C, F = mesh.shape["ctx"], mesh.shape["fsdp"]
    wide = P("fsdp", "ctx", "tp")
    return jax.shard_map(
        functools.partial(mixer, C, F, True),
        mesh=mesh,
        in_specs=(wide, wide, wide, wide, P("fsdp", "ctx"), P("tp", "fsdp"), P(None, None, "tp")),
        out_specs=(wide, wide, wide, P("tp", "fsdp"), P(None, None, "tp")),
        check_vma=False,
    )
```

```python
import functools
import math

import jax
import jax.numpy as jnp
from jax import lax
from jax.experimental import pallas as pl
from jax.experimental.pallas import tpu as pltpu
from jax.sharding import PartitionSpec as P

TAPS = 128
SHORT = 7
LANES = 128
PAD = 8
TAIL = 16
CHUNK = 32
F32 = jnp.float32
BF16 = jnp.bfloat16
MESH = pl.DeviceIdType.MESH
NT_DIMS = (((1,), (1,)), ((), ()))

TAILS, IDS_DOWN, IDS_UP, U_HALO, DZ_HALO, HEADS, FILTERS = 0, 3, 4, 5, 6, 7, 10
SCATTER, EXCHANGE, GATHER, SLOTS = 11, 14, 17, 20
STREAMS = 3
CORES = 2


def kernel(
    dims,
    q_hbm, k_hbm, v_hbm, g_hbm, ids_hbm, lf_hbm, sf_hbm,
    oq_hbm, ok_hbm, ov_hbm, ogl_ref, ogs_ref,
    xin_ref, g_ref, ids_ref, lf_ref, sf_ref, out_ref,
    x32, pm_ref, ks_ref, vs_ref, u_ref, dz_ref, uh_ref, dzh_ref, ut_ref, dzt_ref,
    tails_ref, idp_ref, idn_ref,
    lfs_ref, h_ref, hn_ref, ba_ref, bc_ref, mc_ref, ma_ref, mq_ref, idc_ref, ms_ref, mas_ref,
    d32, dh_ref, gl_ref, turn_ref, turned_ref, *rest,
):
    pay_refs, rs_refs, red_refs, fin_refs = (rest[n * STREAMS:(n + 1) * STREAMS] for n in range(4))
    ssem, rsem, isem, osem = rest[4 * STREAMS:]
    C, F, remote = dims
    R = xin_ref.shape[1]
    T = xin_ref.shape[2] // LANES
    B = R // TAPS
    tapw, G = lf_ref.shape
    GT = G // T
    width = LANES // GT
    pers = [tiles // (min(4, F) * CORES) for tiles in (2 * T, T, T)]
    ctx = lax.axis_index("ctx") if remote else 0
    fs = lax.axis_index("fsdp") if remote else 0
    nxt = {"ctx": lax.rem(ctx + 1, C)}
    prv = {"ctx": lax.rem(ctx + C - 1, C)}
    XS = min(4, F)
    ZS, YS = F // XS, C // CORES
    z, x, y, core = fs // XS, fs % XS, ctx // CORES, ctx % CORES
    near_count, far_count = XS * CORES, ZS * YS
    near, far = x * CORES + core, z * YS + y
    ring = lambda d, n: min(d, n - d)
    fs_order = sorted(range(1, F), key=lambda d: -ring(d % XS, XS) - 4 * (d >= XS))
    near_order = sorted(range(1, near_count), key=lambda d: -ring(d, near_count))
    far_order = [(dz, dy) for dz in range(ZS) for dy in range(YS) if dz or dy]
    far_order.sort(key=lambda p: -ring(p[1], YS) - 4 * p[0])

    def rcopy(src, dst, slot, device):
        return pltpu.make_async_remote_copy(
            src_ref=src, dst_ref=dst, send_sem=ssem.at[slot], recv_sem=rsem.at[slot],
            device_id=device, device_id_type=MESH,
        )

    def whole(ref, slot):
        return rcopy(ref, ref, slot, prv)

    def near_peer(d):
        index = (near + d) % near_count
        return index, {"fsdp": z * XS + index // CORES, "ctx": y * CORES + index % CORES}

    def far_peer(dz, dy):
        return {"fsdp": (z + dz) % ZS * XS + x, "ctx": (y + dy) % YS * CORES + core}

    def fs_peer(d):
        return lax.rem(fs + d, F)

    if remote:
        barrier = pltpu.get_barrier_semaphore()
        for d in fs_order:
            pl.semaphore_signal(barrier, inc=1, device_id={"fsdp": fs_peer(d)}, device_id_type=MESH)
        greeted = [far_peer(dz, dy) for dz, dy in far_order if dy]
        greeted += [
            {"fsdp": z * XS + (x + dx) % XS, "ctx": y * CORES + 1 - core} for dx in range(XS)
        ]
        greeted.append({"ctx": (ctx + 2 * core - 1 + C) % C})
        for device in greeted:
            pl.semaphore_signal(barrier, inc=1, device_id=device, device_id_type=MESH)

    early = (T + 1) // 2
    half = early * LANES
    wide_loads = [
        (src.at[0, :, lanes], dst.at[:, lanes])
        for lanes in (pl.ds(0, half), pl.ds(half, T * LANES - half))
        for src, dst in (
            (q_hbm, xin_ref.at[0]), (k_hbm, xin_ref.at[1]), (v_hbm, xin_ref.at[2]), (g_hbm, g_ref),
        )
    ]
    loads = [
        pltpu.make_async_copy(src, dst, isem.at[n])
        for n, (src, dst) in enumerate(
            [(ids_hbm, ids_ref), (sf_hbm, sf_ref)] + wide_loads + [(lf_hbm, lf_ref)]
        )
    ]
    for load in loads:
        load.start()
    loads[0].wait()

    def fill_columns(row, chunk):
        idc_ref[chunk * LANES:(chunk + 1) * LANES, :] = jnp.transpose(
            jnp.broadcast_to(row, (LANES, LANES))
        )

    own_ids = ids_ref[...].astype(F32)
    for b in range(B):
        fill_columns(own_ids[:, b * LANES:(b + 1) * LANES], 1 + b)

    def fill_short_masks(r0, n):
        here = idc_ref[pl.ds(LANES + r0, n), :]
        for j in range(1, SHORT):
            back = idc_ref[pl.ds(LANES + r0 - j, n), :]
            ms_ref[j - 1, pl.ds(r0, n), :] = jnp.where(here == back, 1.0, 0.0)

    fill_short_masks(TAIL, R - TAIL)

    def lane_block(t):
        return pl.ds(pl.multiple_of(t * LANES, LANES), LANES)

    for load in loads[1:6]:
        load.wait()

    def widen(t, carry):
        for i in range(3):
            x32[i, t, PAD:PAD + R, :] = xin_ref[i, :, lane_block(t)].astype(F32)
        return carry

    def short_rows(t, r0, n):
        convs = []
        for i in range(3):
            total = x32[i, t, pl.ds(PAD + r0, n), :] * sf_ref[i, 0:1, lane_block(t)]
            for j in range(1, SHORT):
                piece = x32[i, t, pl.ds(PAD + r0 - j, n), :] * ms_ref[j - 1, pl.ds(r0, n), :]
                pm_ref[i, j - 1, t, pl.ds(r0, n), :] = piece
                total = total + piece * sf_ref[i, j:j + 1, lane_block(t)]
            convs.append(total)
        qs, ks, vs = convs
        ks_ref[t, pl.ds(r0, n), :] = ks
        vs_ref[t, pl.ds(r0, n), :] = vs
        u_ref[t, pl.ds(r0, n), :] = (ks * vs).astype(BF16)
        upstream = g_ref[pl.ds(r0, n), lane_block(t)].astype(F32)
        dz_ref[t, pl.ds(r0, n), :] = (upstream * qs).astype(BF16)

    def short_main(t, carry):
        widen(t, carry)
        short_rows(t, TAIL, CHUNK - TAIL)
        for r0 in range(CHUNK, R, CHUNK):
            short_rows(t, r0, CHUNK)
        return carry

    lax.fori_loop(0, early, short_main, 0)

    for load in loads[6:]:
        load.wait()
    if remote:
        pl.semaphore_wait(barrier, len(greeted) + F - 1)
        filter_sends = [
            rcopy(lf_ref, lfs_ref.at[fs], FILTERS, {"fsdp": fs_peer(d)}) for d in fs_order
        ]
        tail_copies = [
            rcopy(xin_ref.at[i, pl.ds(R - TAIL, TAIL), :], tails_ref.at[i], TAILS + i, nxt)
            for i in range(3)
        ]
        ids_down = rcopy(ids_ref, idp_ref, IDS_DOWN, nxt)
        ids_up = rcopy(ids_ref, idn_ref, IDS_UP, prv)
        for copy in filter_sends + [ids_down, ids_up] + tail_copies:
            copy.start()
    lfs_ref[fs] = lf_ref[...]
    lax.fori_loop(early, T, short_main, 0)

    if remote:
        u_copy = rcopy(u_ref.at[:, pl.ds(R - TAPS, TAPS), :], uh_ref, U_HALO, nxt)
        u_copy.start()
        for copy in tail_copies + [ids_down, ids_up]:
            copy.wait()

    prev_ids = idp_ref[...].astype(F32)[:, R - LANES:]
    next_ids = idn_ref[...].astype(F32)[:, :LANES]
    if remote:
        prev_ids = jnp.where(ctx == 0, -1.0, prev_ids)
        next_ids = jnp.where(ctx == C - 1, -1.0, next_ids)
    fill_columns(prev_ids, 0)
    fill_columns(next_ids, 1 + B)
    fill_short_masks(0, TAIL)

    def short_head(t, carry):
        for i in range(3):
            x32[i, t, 0:PAD, :] = tails_ref[i, :, lane_block(t)].astype(F32)[TAIL - PAD:]
        short_rows(t, 0, TAIL)
        return carry

    lax.fori_loop(0, T, short_head, 0)

    if remote:
        dz_copy = rcopy(dz_ref.at[:, pl.ds(0, TAPS), :], dzh_ref, DZ_HALO, prv)
        dz_copy.start()

    for j in range(1, SHORT):
        ahead = idc_ref[pl.ds(LANES + j, R), :]
        mas_ref[j - 1] = jnp.where(idc_ref[pl.ds(LANES, R), :] == ahead, 1.0, 0.0)
    rows = [prev_ids] + [own_ids[:, b * LANES:(b + 1) * LANES] for b in range(B)] + [next_ids]
    row_index = lax.broadcasted_iota(jnp.int32, (TAPS, LANES), 0)
    col_index = lax.broadcasted_iota(jnp.int32, (TAPS, LANES), 1)
    one = jnp.ones((TAPS, LANES), F32)
    zero = jnp.zeros((TAPS, LANES), F32)
    upper = jnp.where(col_index >= row_index, one, zero)
    above = jnp.where(col_index > row_index, one, zero)
    for b in range(B):
        column = idc_ref[(1 + b) * LANES:(2 + b) * LANES, :]
        same = [jnp.where(column == rows[b + n], one, zero) for n in range(3)]
        mc_ref[b, :, :LANES] = (same[0] * above).astype(BF16)
        mc_ref[b, :, LANES:] = (same[1] * (one - above)).astype(BF16)
        ma_ref[b, :, :LANES] = (same[1] * upper).astype(BF16)
        ma_ref[b, :, LANES:] = (same[2] * (one - upper)).astype(BF16)
        mq_ref[b] = same[1] * upper + same[2] * (one - upper)

    def dz_window(t, b):
        if b + 1 < B:
            return dz_ref[t, b * TAPS:(b + 2) * TAPS, :]
        return jnp.concatenate([dz_ref[t, b * TAPS:, :], dzh_ref[t]], axis=0)

    lane_row = lax.broadcasted_iota(jnp.int32, (1, LANES), 1) // width
    group_lanes = [jnp.where(lane_row == g, 1.0, 0.0).astype(BF16) for g in range(GT)]
    in_upper = col_index >= row_index

    def long_grad(t, b):
        signal = u_ref[t, b * TAPS:(b + 1) * TAPS, :]
        left = jnp.concatenate([signal * group_lanes[g] for g in range(GT)], axis=0)
        product = lax.dot_general(left, dz_window(t, b), NT_DIMS, preferred_element_type=F32)
        mask = mq_ref[b]
        parts = []
        for g in range(GT):
            part = product[g * TAPS:(g + 1) * TAPS]
            parts.append(jnp.where(in_upper, part[:, :LANES], part[:, LANES:]) * mask)
        return parts

    def early_grad(t, carry):
        for b in range(B - 1):
            for g, part in enumerate(long_grad(t, b)):
                gl_ref[t * GT + g] = part if b == 0 else gl_ref[t * GT + g] + part
        return carry

    lax.fori_loop(0, T, early_grad, 0, unroll=8)

    def turn_own(t, carry):
        for b in range(B):
            ut_ref[t, 1 + b] = jnp.transpose(u_ref[t, b * TAPS:(b + 1) * TAPS, :])
            dzt_ref[t, b] = jnp.transpose(dz_ref[t, b * TAPS:(b + 1) * TAPS, :])
        return carry

    lax.fori_loop(0, T, turn_own, 0, unroll=4)

    if remote:
        whole(lfs_ref.at[pl.ds(0, F - 1)], FILTERS).wait_recv()
    stacked = jnp.concatenate([lfs_ref[s] for s in range(F)], axis=0)
    unit_row = lax.broadcasted_iota(jnp.int32, (G, G), 0)
    unit_col = lax.broadcasted_iota(jnp.int32, (G, G), 1)
    unit = jnp.where(unit_row == unit_col, 1.0, 0.0).astype(BF16)
    taps = lax.dot_general(unit, stacked, NT_DIMS, preferred_element_type=F32)
    swap = jnp.where(((row_index + col_index) & (TAPS - 1)) == 0, 1.0, 0.0).astype(BF16)
    h_ref[...] = taps
    hn_ref[...] = jnp.dot(taps.astype(BF16), swap, preferred_element_type=F32)
    sub = lax.broadcasted_iota(jnp.int32, (8, TAPS), 0)
    unroll = 8

    def band_of(row):
        base = jnp.broadcast_to(row, (8, TAPS))
        for bit in (1, 2, 4):
            base = jnp.where((sub & bit) != 0, pltpu.roll(base, bit, 1), base)
        parts = [base] + [pltpu.roll(base, 8 * a, 1) for a in range(1, TAPS // 8)]
        return jnp.concatenate(parts, axis=0).astype(BF16)

    def build(n, carry):
        for m in range(unroll):
            g = n * unroll + m
            for band_ref, row_ref in ((ba_ref, h_ref), (bc_ref, hn_ref)):
                band = band_of(row_ref[pl.ds(g, 1), :])
                band_ref[g] = jnp.concatenate([band, band], axis=1)
        return carry

    lax.fori_loop(0, G // unroll, build, 0)

    def banded(band_ref, mask_ref, b, t, left_ref, first):
        parts = []
        for g in range(GT):
            band = band_ref[t * GT + g]
            weights = band * mask_ref[b]
            rows_g = slice(g * width, (g + 1) * width)
            left = jnp.concatenate([left_ref[t, first, rows_g, :], left_ref[t, first + 1, rows_g, :]], axis=1)
            parts.append(lax.dot_general(left, weights, NT_DIMS, preferred_element_type=F32))
        return jnp.transpose(jnp.concatenate(parts, axis=0))

    def backward_rows(t, b):
        here = pl.ds(b * TAPS, TAPS)
        du = banded(ba_ref, ma_ref, b, t, dzt_ref, b)
        d32[1, t, here, :] = du * vs_ref[t, here, :]
        d32[2, t, here, :] = du * ks_ref[t, here, :]

    def forward_rows(t, b):
        here = pl.ds(b * TAPS, TAPS)
        z = banded(bc_ref, mc_ref, b, t, ut_ref, b)
        d32[0, t, here, :] = g_ref[here, lane_block(t)].astype(F32) * z

    def inner_products(t, carry):
        for b in range(B - 1):
            backward_rows(t, b)
        for b in range(1, B):
            forward_rows(t, b)
        return carry

    lax.fori_loop(0, T, inner_products, 0, unroll=8)

    positions = C * F * R
    long_scale = 1.0 / math.sqrt(positions * width)
    short_scale = 1.0 / math.sqrt(positions)

    def short_grad(t, i):
        grads = d32[i, t, 0:R, :]
        sums = []
        for j in range(SHORT):
            source = pm_ref[i, j - 1, t] if j else x32[i, t, PAD:PAD + R, :]
            sums.append(jnp.sum(grads * source, axis=0, keepdims=True))
        sums.append(jnp.zeros((1, LANES), F32))
        return jnp.concatenate(sums, axis=0) * short_scale

    if remote:
        dz_copy.wait()

    def last_backward(t, carry):
        dzt_ref[t, B] = jnp.transpose(dzh_ref[t])
        backward_rows(t, B - 1)
        for i in (1, 2):
            pay_refs[0][(i - 1) * T + t] = short_grad(t, i)
        return carry

    lax.fori_loop(0, T, last_backward, 0, unroll=8)

    def heads(i):
        return rcopy(d32.at[i, :, pl.ds(0, PAD), :], dh_ref.at[i], HEADS + i, prv)

    def own_slots(n, owner):
        return pl.ds(owner * pers[n], pers[n])

    def scatter(n):
        for d in near_order:
            index, device = near_peer(d)
            rcopy(pay_refs[n].at[own_slots(n, index)], rs_refs[n].at[near], SCATTER + n, device).start()
        rs_refs[n][near] = pay_refs[n][own_slots(n, near)]

    def sum_scattered(n):
        whole(rs_refs[n].at[pl.ds(0, near_count - 1)], SCATTER + n).wait_recv()
        total = rs_refs[n][0]
        for c in range(1, near_count):
            total = total + rs_refs[n][c]
        own = red_refs[n].at[far]
        own[...] = total
        for dz, dy in far_order:
            rcopy(own, own, EXCHANGE + n, far_peer(dz, dy)).start()

    if remote:
        scatter(0)
        heads(1).start()
        heads(2).start()

    sub_all = lax.broadcasted_iota(jnp.int32, (GT * 8, TAPS), 0) & 7

    def late_grad(t, carry):
        folded = []
        for g, part in enumerate(long_grad(t, B - 1)):
            if B > 1:
                part = part + gl_ref[t * GT + g]
            total = part[0:8]
            for a in range(1, TAPS // 8):
                total = total + pltpu.roll(part[8 * a:8 * a + 8], LANES - 8 * a, 1)
            folded.append(total)
        stack = jnp.concatenate(folded, axis=0)
        for bit in (1, 2, 4):
            stack = jnp.where((sub_all & bit) != 0, pltpu.roll(stack, LANES - bit, 1), stack)
        pay_refs[1][t] = jnp.sum(stack.reshape(GT, 8, TAPS), axis=1) * long_scale
        return carry

    lax.fori_loop(0, T, late_grad, 0, unroll=8)
    if remote:
        scatter(1)
        sum_scattered(0)
        u_copy.wait()

    def last_forward(t, carry):
        ut_ref[t, 0] = jnp.transpose(uh_ref[t])
        forward_rows(t, 0)
        pay_refs[2][t] = short_grad(t, 0)
        return carry

    lax.fori_loop(0, T, last_forward, 0, unroll=8)
    if remote:
        scatter(2)
        heads(0).start()
        sum_scattered(1)

    def outputs(i, o_hbm):
        if remote:
            heads(i).wait_recv()
        d32[i, :, R:R + PAD, :] = dh_ref[i]

        def one_block(t, carry):
            total = d32[i, t, pl.ds(0, R), :] * sf_ref[i, 0:1, lane_block(t)]
            for j in range(1, SHORT):
                piece = d32[i, t, pl.ds(j, R), :] * mas_ref[j - 1]
                total = total + piece * sf_ref[i, j:j + 1, lane_block(t)]
            out_ref[i, :, lane_block(t)] = total.astype(BF16)
            return carry

        lax.fori_loop(0, T, one_block, 0)
        pltpu.make_async_copy(out_ref.at[i], o_hbm.at[0], osem.at[i]).start()

    def sum_exchanged(n):
        whole(red_refs[n].at[pl.ds(0, far_count - 1)], EXCHANGE + n).wait_recv()
        total = red_refs[n][0]
        for f in range(1, far_count):
            total = total + red_refs[n][f]
        own = fin_refs[n].at[own_slots(n, near)]
        own[...] = total
        for d in near_order:
            rcopy(own, own, GATHER + n, near_peer(d)[1]).start()

    def others(n):
        return fin_refs[n].at[pl.ds(0, (near_count - 1) * pers[n])]

    outputs(1, ok_hbm)
    if remote:
        sum_scattered(2)
    outputs(2, ov_hbm)
    if remote:
        sum_exchanged(0)
    outputs(0, oq_hbm)
    if remote:
        sum_exchanged(1)
        sum_exchanged(2)
        for n in range(STREAMS):
            whole(others(n), GATHER + n).wait_recv()
    for t in range(T):
        lanes = slice(t * LANES, (t + 1) * LANES)
        ogs_ref[0, :, lanes] = fin_refs[2][t, 0:SHORT, :]
        ogs_ref[1, :, lanes] = fin_refs[0][t, 0:SHORT, :]
        ogs_ref[2, :, lanes] = fin_refs[0][T + t, 0:SHORT, :]
    if G < LANES:
        turn_ref[G:, :] = jnp.zeros((LANES - G, TAPS), F32)
    for t in range(T):
        turn_ref[GT * t:GT * t + GT, :] = fin_refs[1][t]
    turned_ref[...] = jnp.transpose(turn_ref[...])
    ogl_ref[...] = turned_ref[pl.ds(pl.multiple_of(fs * tapw, 8), tapw), :][:, :G]
    for i, o_hbm in enumerate((oq_hbm, ok_hbm, ov_hbm)):
        pltpu.make_async_copy(out_ref.at[i], o_hbm.at[0], osem.at[i]).wait()
    if remote:
        whole(lfs_ref.at[pl.ds(0, F - 1)], FILTERS).wait_send()
        for i in range(3):
            heads(i).wait_send()
        for n in range(STREAMS):
            whole(rs_refs[n].at[pl.ds(0, near_count - 1)], SCATTER + n).wait_send()
            whole(red_refs[n].at[pl.ds(0, far_count - 1)], EXCHANGE + n).wait_send()
            whole(others(n), GATHER + n).wait_send()


def settle(*refs):
    count = (len(refs) - 2) // 3
    sources, targets, held = refs[:count], refs[count:2 * count], refs[2 * count:3 * count]
    in_sem, out_sem = refs[3 * count:]
    loads = [pltpu.make_async_copy(a, b, in_sem.at[n]) for n, (a, b) in enumerate(zip(sources, held))]
    stores = [pltpu.make_async_copy(a, b, out_sem.at[n]) for n, (a, b) in enumerate(zip(held, targets))]
    for load in loads:
        load.start()
    for load, store in zip(loads, stores):
        load.wait()
        store.start()
    for store in stores:
        store.wait()


def settled(arrays):
    anywhere = [pl.BlockSpec(memory_space=pl.ANY)] * len(arrays)
    shapes = [jax.ShapeDtypeStruct(a.shape, a.dtype) for a in arrays]
    return pl.pallas_call(
        settle,
        out_shape=shapes,
        in_specs=anywhere,
        out_specs=anywhere,
        scratch_shapes=[pltpu.VMEM(a.shape, a.dtype) for a in arrays]
        + [pltpu.SemaphoreType.DMA((len(arrays),))] * 2,
        compiler_params=pltpu.CompilerParams(vmem_limit_bytes=60 * 1024 * 1024),
        name="settle",
    )(*arrays)


def mixer(C, F, remote, q_in, k_in, v_in, grad_out, ids, long_filter, short_filter):
    R, channels = q_in.shape[1], q_in.shape[2]
    T, B = channels // LANES, R // TAPS
    G, tapw = long_filter.shape
    wide = jax.ShapeDtypeStruct(q_in.shape, BF16)
    streams = (2 * T, T, T)
    near = min(4, F) * CORES
    far = C * F // near
    vmem = pltpu.VMEM
    blocks = (T, TAPS, LANES)
    results = pl.pallas_call(
        functools.partial(kernel, (C, F, remote)),
        out_shape=(
            wide, wide, wide,
            jax.ShapeDtypeStruct((tapw, G), F32),
            jax.ShapeDtypeStruct(short_filter.shape, F32),
        ),
        in_specs=[pl.BlockSpec(memory_space=pl.ANY)] * 7,
        out_specs=[pl.BlockSpec(memory_space=pl.ANY)] * 3 + [pl.BlockSpec(memory_space=vmem)] * 2,
        scratch_shapes=[
            vmem((3, R, channels), BF16), vmem((R, channels), BF16),
            vmem((1, R), jnp.int32), vmem((tapw, G), BF16), vmem(short_filter.shape, F32),
            vmem((3, R, channels), BF16),
            vmem((3, T, PAD + R, LANES), F32),
            vmem((3, SHORT - 1, T, R, LANES), F32),
            vmem((T, R, LANES), F32), vmem((T, R, LANES), F32),
            vmem((T, R, LANES), BF16), vmem((T, R, LANES), BF16),
            vmem(blocks, BF16), vmem(blocks, BF16),
            vmem((T, B + 1, LANES, TAPS), BF16), vmem((T, B + 1, LANES, TAPS), BF16),
            vmem((3, TAIL, channels), BF16),
            vmem((1, R), jnp.int32), vmem((1, R), jnp.int32),
            vmem((F, tapw, G), BF16),
            vmem((G, TAPS), F32), vmem((G, TAPS), F32),
            vmem((G, TAPS, 2 * TAPS), BF16), vmem((G, TAPS, 2 * TAPS), BF16),
            vmem((B, TAPS, 2 * LANES), BF16), vmem((B, TAPS, 2 * LANES), BF16),
            vmem((B, TAPS, LANES), F32),
            vmem((R + 2 * LANES, LANES), F32),
            vmem((SHORT - 1, R, LANES), F32), vmem((SHORT - 1, R, LANES), F32),
            vmem((3, T, R + PAD, LANES), F32),
            vmem((3, T, PAD, LANES), F32),
            vmem((G, TAPS, LANES), F32),
            vmem((TAPS, LANES), F32), vmem((TAPS, LANES), F32),
            *(vmem((tiles, 8, LANES), F32) for tiles in streams),
            *(vmem((near, tiles // near, 8, LANES), F32) for tiles in streams),
            *(vmem((far, tiles // near, 8, LANES), F32) for tiles in streams),
            *(vmem((tiles, 8, LANES), F32) for tiles in streams),
            pltpu.SemaphoreType.DMA((SLOTS,)),
            pltpu.SemaphoreType.DMA((SLOTS,)),
            pltpu.SemaphoreType.DMA((11,)),
            pltpu.SemaphoreType.DMA((3,)),
        ],
        compiler_params=pltpu.CompilerParams(
            collective_id=0 if remote else None,
            has_side_effects=True,
            vmem_limit_bytes=60 * 1024 * 1024,
        ),
        name="mixer",
    )(q_in, k_in, v_in, grad_out, ids, long_filter.T, short_filter)
    *grads, grad_long, grad_short = settled(results)
    return (*grads, grad_long.T, grad_short)


def solution(mesh):
    C, F = mesh.shape["ctx"], mesh.shape["fsdp"]
    wide = P("fsdp", "ctx", "tp")
    return jax.shard_map(
        functools.partial(mixer, C, F, True),
        mesh=mesh,
        in_specs=(wide, wide, wide, wide, P("fsdp", "ctx"), P("tp", "fsdp"), P(None, None, "tp")),
        out_specs=(wide, wide, wide, P("tp", "fsdp"), P(None, None, "tp")),
        check_vma=False,
    )
```
